32 devices in a mesh: ctx: 8 (over z, y), head: 4 (over x, core).
Axes of the slice: x: 2, y: 2, z: 4, core: 2. Of those that a mesh axis runs over, the one named last changes fastest.
Arguments:
- queries: bfloat16 [4096, 4096], P(('ctx', 'head')), may hold values from -6 to 6
- keys: bfloat16 [4096, 1024], P(('ctx', 'head')), may hold values from -6 to 6
- values: bfloat16 [4096, 1024], P(('ctx', 'head')), may hold values from -6 to 6
- cotangent: bfloat16 [4096, 4096], P(('ctx', 'head')), may hold values from -6 to 6
Outputs:
- out: bfloat16 [4096, 4096], P(('ctx', 'head'))
- grad_queries: bfloat16 [4096, 4096], P(('ctx', 'head'))
- grad_keys: bfloat16 [4096, 1024], P(('ctx', 'head'))
- grad_values: bfloat16 [4096, 1024], P(('ctx', 'head'))
The draws below stay inside these ranges and needn't reach their ends.
All inputs are finite; a program needn't handle non-finite values.
Results may differ from the reference program's by a relative error of at most 0.008.
Values may be sent and summed in bfloat16 or wider, within the bound.
No kernel may reach another device: no remote copies, remote signals or barrier semaphores. Data moves between devices by JAX's collectives and lax.ppermute only.
A program may use at most 64 MiB of HBM per device.

```python
from functools import partial
import jax
import jax.numpy as jnp
from jax import lax

QUERY_HEADS = 32
KEY_VALUE_HEADS = 8
HEAD_FEATURES = 128
BLOCK_POSITIONS = 512
BLOCK_COUNT = 8
SEQUENCE_LENGTH = 4096


def draw_queries(key, part):
    layer_output = jax.random.normal(jax.random.fold_in(key, 3), (SEQUENCE_LENGTH, QUERY_HEADS, HEAD_FEATURES), jnp.float32)
    return jnp.clip(layer_output, -6.0, 6.0).reshape(SEQUENCE_LENGTH, QUERY_HEADS * HEAD_FEATURES).astype(jnp.bfloat16)


def draw_keys(key, part):
    random_noise = jax.random.normal(jax.random.fold_in(key, 1), (BLOCK_COUNT, BLOCK_POSITIONS, KEY_VALUE_HEADS, HEAD_FEATURES), jnp.float32)
    start_offset = 2.0 * jax.random.normal(jax.random.fold_in(key, 2), (BLOCK_COUNT, 1, KEY_VALUE_HEADS, HEAD_FEATURES), jnp.float32)
    layer_output = (random_noise + start_offset).reshape(SEQUENCE_LENGTH, KEY_VALUE_HEADS, HEAD_FEATURES)
    return jnp.clip(layer_output, -6.0, 6.0).reshape(SEQUENCE_LENGTH, KEY_VALUE_HEADS * HEAD_FEATURES).astype(jnp.bfloat16)


def draw_values(key, part):
    random_noise = jax.random.normal(jax.random.fold_in(key, 6), (BLOCK_COUNT, BLOCK_POSITIONS, KEY_VALUE_HEADS, HEAD_FEATURES), jnp.float32)
    start_offset = jax.random.normal(jax.random.fold_in(key, 7), (BLOCK_COUNT, 1, KEY_VALUE_HEADS, HEAD_FEATURES), jnp.float32)
    layer_output = random_noise + start_offset
    return jnp.clip(layer_output, -6.0, 6.0).reshape(SEQUENCE_LENGTH, KEY_VALUE_HEADS * HEAD_FEATURES).astype(jnp.bfloat16)


def levels(rng, extent, cuts, least, high):
    def one(dim, shards_of):
        steps = jax.random.uniform(jax.random.fold_in(jax.random.fold_in(rng, 6), dim), (shards_of,), jnp.float32, least / len(cuts), high / len(cuts))
        return jnp.repeat(jnp.exp(steps), extent[dim] // shards_of).reshape((-1,) + (1,) * (len(extent) - dim - 1))

    gain = one(*cuts[0])
    for cut in cuts[1:]:
        gain = gain * one(*cut)
    return gain


def centred(own_key, shape, scale, most, cuts=(), held_as=jnp.bfloat16):
    entries = jax.random.normal(own_key, shape, jnp.float32) * scale
    if len(cuts) > 0:
        entries = levels(own_key, shape, cuts, -0.22, 0.18) * entries
    return jnp.clip(entries, min=-most, max=most).astype(held_as)


def setup_inputs(seed: int = 0) -> dict:
    key_list = jax.random.split(jax.random.key(seed), 5)
    queries = draw_queries(jax.random.fold_in(key_list[4], 71), 0)
    keys = draw_keys(jax.random.fold_in(key_list[4], 71), 0)
    values = draw_values(jax.random.fold_in(key_list[4], 71), 0)
    cotangent = centred(key_list[3], (SEQUENCE_LENGTH, QUERY_HEADS * HEAD_FEATURES), 1.0, 6.0, ((0, 32),))
    return dict(queries=queries, keys=keys, values=values, cotangent=cotangent)


LOWEST = -1e30


def head_terms(query, grad_out, band_keys, band_values, block_summary_keys, block_summary_values, first, keep):
    row_count = query.shape[0]
    width = band_keys.shape[0]
    scale = query.shape[1] ** -0.5
    query_pos = first + jnp.arange(row_count, dtype=jnp.int32)
    key_pos = first - (width - row_count) + jnp.arange(width, dtype=jnp.int32)
    band_mask = (key_pos[None, :] >= 0) & (key_pos[None, :] <= query_pos[:, None])
    summary_mask = jnp.arange(block_summary_keys.shape[0], dtype=jnp.int32)[None, :] < (first // BLOCK_POSITIONS)
    band_score = jnp.dot(query, band_keys.T, preferred_element_type=jnp.float32) * scale
    summary_score = jnp.dot(query, block_summary_keys.T, preferred_element_type=jnp.float32) * scale
    row_top = jnp.maximum(jnp.max(jnp.where(band_mask, band_score, LOWEST), axis=1),
                          jnp.max(jnp.where(summary_mask, summary_score, LOWEST), axis=1))
    band_weight = jnp.where(band_mask, jnp.exp(band_score - row_top[:, None]), 0.0)
    summary_weight = jnp.where(summary_mask, jnp.exp(summary_score - row_top[:, None]), 0.0)
    row_total = jnp.sum(band_weight, axis=1) + jnp.sum(summary_weight, axis=1)
    band_prob = band_weight / row_total[:, None]
    summary_prob = summary_weight / row_total[:, None]
    band_low = band_prob.astype(jnp.bfloat16)
    summary_low = summary_prob.astype(jnp.bfloat16)
    attended = jnp.dot(band_low, band_values, preferred_element_type=jnp.float32) + jnp.dot(summary_low, block_summary_values, preferred_element_type=jnp.float32)
    row_dot = jnp.sum(grad_out.astype(jnp.float32) * attended, axis=1)
    band_back = jnp.dot(grad_out, band_values.T, preferred_element_type=jnp.float32)
    summary_back = jnp.dot(grad_out, block_summary_values.T, preferred_element_type=jnp.float32)
    band_slope = (band_prob * (band_back - row_dot[:, None])).astype(jnp.bfloat16)
    summary_slope = (summary_prob * (summary_back - row_dot[:, None])).astype(jnp.bfloat16)
    grad_query = (jnp.dot(band_slope, band_keys, preferred_element_type=jnp.float32) + jnp.dot(summary_slope, block_summary_keys, preferred_element_type=jnp.float32)) * scale
    grad_key = jnp.dot(band_slope[:, width - keep:].T, query, preferred_element_type=jnp.float32) * scale
    grad_value = jnp.dot(band_low[:, width - keep:].T, grad_out, preferred_element_type=jnp.float32)
    grad_sum_key = jnp.dot(summary_slope.T, query, preferred_element_type=jnp.float32) * scale
    grad_sum_value = jnp.dot(summary_low.T, grad_out, preferred_element_type=jnp.float32)
    return attended, grad_query, grad_key, grad_value, grad_sum_key, grad_sum_value, row_top, row_total, row_dot


def combine_blocks(band_all, summary_total):
    own = band_all[:, :, BLOCK_POSITIONS:]
    later = jnp.concatenate([band_all[1:, :, :BLOCK_POSITIONS], jnp.zeros_like(band_all[:1, :, :BLOCK_POSITIONS])], axis=0)
    spread = summary_total.transpose(1, 0, 2)[:, :, None, :] / BLOCK_POSITIONS
    grand_total = own + later + spread
    return grand_total.transpose(0, 2, 1, 3).reshape(SEQUENCE_LENGTH, KEY_VALUE_HEADS * HEAD_FEATURES).astype(jnp.bfloat16)


def reference(queries, keys, values, cotangent):
    head_count = QUERY_HEADS // KEY_VALUE_HEADS
    query_blocks = queries.reshape(BLOCK_COUNT, BLOCK_POSITIONS, QUERY_HEADS, HEAD_FEATURES)
    scaled_blocks = (cotangent * 16).astype(jnp.bfloat16).reshape(BLOCK_COUNT, BLOCK_POSITIONS, QUERY_HEADS, HEAD_FEATURES)
    token_keys = keys.reshape(SEQUENCE_LENGTH, KEY_VALUE_HEADS, HEAD_FEATURES)
    token_values = values.reshape(SEQUENCE_LENGTH, KEY_VALUE_HEADS, HEAD_FEATURES)
    block_summary_keys = (jnp.sum(token_keys.reshape(BLOCK_COUNT, BLOCK_POSITIONS, KEY_VALUE_HEADS, HEAD_FEATURES), axis=1, dtype=jnp.float32) / BLOCK_POSITIONS).astype(jnp.bfloat16)
    block_summary_values = (jnp.sum(token_values.reshape(BLOCK_COUNT, BLOCK_POSITIONS, KEY_VALUE_HEADS, HEAD_FEATURES), axis=1, dtype=jnp.float32) / BLOCK_POSITIONS).astype(jnp.bfloat16)
    summary_key_heads = jnp.repeat(block_summary_keys.transpose(1, 0, 2), head_count, axis=0)
    summary_value_heads = jnp.repeat(block_summary_values.transpose(1, 0, 2), head_count, axis=0)
    pad_amount = jnp.zeros((BLOCK_POSITIONS, KEY_VALUE_HEADS, HEAD_FEATURES), jnp.bfloat16)
    padded_keys = jnp.concatenate([pad_amount, token_keys], axis=0)
    padded_values = jnp.concatenate([pad_amount, token_values], axis=0)

    def step_block(carry, block):
        key_running_sum, value_running_sum = carry
        first = block * BLOCK_POSITIONS
        band_keys = lax.dynamic_slice_in_dim(padded_keys, first, 2 * BLOCK_POSITIONS, 0)
        band_values = lax.dynamic_slice_in_dim(padded_values, first, 2 * BLOCK_POSITIONS, 0)
        band_key_heads = jnp.repeat(band_keys.transpose(1, 0, 2), head_count, axis=0)
        band_value_heads = jnp.repeat(band_values.transpose(1, 0, 2), head_count, axis=0)
        query_heads = lax.dynamic_index_in_dim(query_blocks, block, 0, keepdims=False).transpose(1, 0, 2)
        grad_heads = lax.dynamic_index_in_dim(scaled_blocks, block, 0, keepdims=False).transpose(1, 0, 2)
        term_list = jax.vmap(partial(head_terms, first=first, keep=2 * BLOCK_POSITIONS))(
            query_heads, grad_heads, band_key_heads, band_value_heads, summary_key_heads, summary_value_heads)
        key_running_sum = key_running_sum + term_list[4].reshape(KEY_VALUE_HEADS, head_count, BLOCK_COUNT, HEAD_FEATURES).sum(axis=1)
        value_running_sum = value_running_sum + term_list[5].reshape(KEY_VALUE_HEADS, head_count, BLOCK_COUNT, HEAD_FEATURES).sum(axis=1)
        local_key_gradient = term_list[2].reshape(KEY_VALUE_HEADS, head_count, 2 * BLOCK_POSITIONS, HEAD_FEATURES).sum(axis=1)
        local_value_gradient = term_list[3].reshape(KEY_VALUE_HEADS, head_count, 2 * BLOCK_POSITIONS, HEAD_FEATURES).sum(axis=1)
        return (key_running_sum, value_running_sum), (term_list[0].astype(jnp.bfloat16), term_list[1].astype(jnp.bfloat16), local_key_gradient, local_value_gradient)

    initial_state = (jnp.zeros((KEY_VALUE_HEADS, BLOCK_COUNT, HEAD_FEATURES), jnp.float32), jnp.zeros((KEY_VALUE_HEADS, BLOCK_COUNT, HEAD_FEATURES), jnp.float32))
    (key_running_sum, value_running_sum), (out_all, grad_query_all, band_key_all, band_value_all) = lax.scan(
        step_block, initial_state, jnp.arange(BLOCK_COUNT, dtype=jnp.int32))
    out = out_all.transpose(0, 2, 1, 3).reshape(SEQUENCE_LENGTH, QUERY_HEADS * HEAD_FEATURES)
    grad_queries = grad_query_all.transpose(0, 2, 1, 3).reshape(SEQUENCE_LENGTH, QUERY_HEADS * HEAD_FEATURES)
    grad_keys = combine_blocks(band_key_all, key_running_sum)
    grad_values = combine_blocks(band_value_all, value_running_sum)
    return (out, grad_queries, grad_keys, grad_values)
```

```python
import jax
import jax.numpy as jnp
from jax import lax
from jax.experimental import pallas as pl
from jax.experimental.pallas import tpu as pltpu
from jax.sharding import PartitionSpec as P

QUERY_HEADS = 32
KEY_VALUE_HEADS = 8
DEPTH = 128
BLOCK = 512
TILE = 256
GROUP = QUERY_HEADS // KEY_VALUE_HEADS
LOWEST = -1e30
LOG2E = 1.4426950408889634

BF = jnp.bfloat16
F32 = jnp.float32


def dot(a, b, ca, cb):
    return lax.dot_general(a, b, (((ca,), (cb,)), ((), ())), preferred_element_type=F32)


def pack_kernel(q_ref, k_ref, v_ref, g_ref, kv_ref, a_ref, b_ref, s_ref):
    half = GROUP * DEPTH
    kv_ref[0, :, : 2 * DEPTH] = k_ref[...]
    kv_ref[0, :, 2 * DEPTH :] = v_ref[...]
    a_ref[0, :, :half] = q_ref[:, :half]
    a_ref[0, :, half:] = g_ref[:, :half]
    b_ref[0, :, :half] = q_ref[:, half:]
    b_ref[0, :, half:] = g_ref[:, half:]
    s_ref[0, :, : 2 * DEPTH] = jnp.sum(k_ref[...].astype(F32), axis=0, keepdims=True)
    s_ref[0, :, 2 * DEPTH :] = jnp.sum(v_ref[...].astype(F32), axis=0, keepdims=True)


def pack(q, k, v, g, parts):
    rows = q.shape[0]
    wide = 2 * GROUP * DEPTH
    return pl.pallas_call(
        pack_kernel,
        grid=(parts,),
        in_specs=[
            pl.BlockSpec((rows, wide), lambda i: (0, i)),
            pl.BlockSpec((rows, 2 * DEPTH), lambda i: (0, i)),
            pl.BlockSpec((rows, 2 * DEPTH), lambda i: (0, i)),
            pl.BlockSpec((rows, wide), lambda i: (0, i)),
        ],
        out_specs=[
            pl.BlockSpec((1, rows, 4 * DEPTH), lambda i: (i, 0, 0)),
            pl.BlockSpec((1, rows, wide), lambda i: (i, 0, 0)),
            pl.BlockSpec((1, rows, wide), lambda i: (i, 0, 0)),
            pl.BlockSpec((1, 1, 4 * DEPTH), lambda i: (i, 0, 0)),
        ],
        out_shape=[
            jax.ShapeDtypeStruct((parts, rows, 4 * DEPTH), BF),
            jax.ShapeDtypeStruct((parts, rows, wide), BF),
            jax.ShapeDtypeStruct((parts, rows, wide), BF),
            jax.ShapeDtypeStruct((parts, 1, 4 * DEPTH), F32),
        ],
        name="pack",
    )(q, k, v, g)


def attend_kernel(
    q_ref, g_ref, k_ref, v_ref, pk_ref, pv_ref, sk_ref, sv_ref,
    o_ref, dq_ref, edge_ref, own_ref, ds_ref,
    kc, vc, kt, vt, dk, dv,
):
    ctx = lax.axis_index("ctx")
    scale = DEPTH ** (-0.5)
    coef = scale * LOG2E
    count = sk_ref.shape[0]
    pad = kc.shape[0] - 2 * BLOCK
    head = pl.program_id(0)

    @pl.when(head == 0)
    def _():
        for ref, all_ref, own, prev, tr in (
            (sk_ref, kc, k_ref, pk_ref, kt),
            (sv_ref, vc, v_ref, pv_ref, vt),
        ):
            mean = (jnp.sum(ref[...], axis=1) * (1.0 / BLOCK)).astype(BF)
            if pad > count:
                mean = jnp.concatenate([mean, jnp.zeros((pad - count, DEPTH), BF)], axis=0)
            all_ref[:pad] = mean
            all_ref[pad : pad + BLOCK] = prev[...]
            all_ref[pad + BLOCK :] = own[...]
            tr[...] = all_ref[...].T
        dk[...] = jnp.zeros_like(dk)
        dv[...] = jnp.zeros_like(dv)

    for tile in range(BLOCK // TILE):
        rows = pl.ds(tile * TILE, TILE)
        edge = pad + BLOCK + TILE * (tile + 1)
        q = q_ref[rows, :]
        s = dot(kc[:edge], q, 1, 1)
        s_sum = s[:pad]
        s_prev = s[pad : pad + BLOCK]
        s_diag = s[edge - TILE :]
        at = lax.broadcasted_iota(jnp.int32, (pad, TILE), 0)
        s_sum = jnp.where(at < ctx, s_sum, LOWEST)
        ki = lax.broadcasted_iota(jnp.int32, (TILE, TILE), 0)
        qi = lax.broadcasted_iota(jnp.int32, (TILE, TILE), 1)
        s_diag = jnp.where(ki <= qi, s_diag, LOWEST)
        pieces = [s_sum, s_prev, s_diag]
        if tile > 0:
            pieces.insert(2, s[pad + BLOCK : edge - TILE])
        tops = [jnp.max(x, axis=0, keepdims=True) for x in pieces]
        tops[1] = jnp.where(ctx > 0, tops[1], LOWEST)
        top = tops[0]
        for x in tops[1:]:
            top = jnp.maximum(top, x)
        shift = [top] * len(pieces)
        shift[1] = jnp.where(ctx > 0, top, -LOWEST)
        weights = [jnp.exp2((x - y) * coef) for x, y in zip(pieces, shift)]
        total = sum(jnp.sum(x, axis=0, keepdims=True) for x in weights)
        inv = 1.0 / total
        weight = jnp.concatenate(weights, axis=0)
        low = weight.astype(BF)
        attended = dot(vt[:, :edge], low, 1, 0) * inv
        o_ref[rows, :] = attended.T.astype(BF)
        gt = (g_ref[rows, :].astype(F32).T * (16.0 * inv)).astype(BF)
        row_dot = jnp.sum(gt.astype(F32) * attended, axis=0, keepdims=True)
        back = dot(vc[:edge], gt, 1, 0)
        slope = (weight * (back - row_dot)).astype(BF)
        dq_ref[rows, :] = (dot(kt[:, :edge], slope, 1, 0) * scale).T.astype(BF)
        dk[:edge] += dot(slope, q, 1, 0)
        dv[:edge] += dot(low, gt, 1, 1)

    @pl.when(head == pl.num_programs(0) - 1)
    def _():
        ds_ref[:, :DEPTH] = dk[:count] * scale
        ds_ref[:, DEPTH:] = dv[:count]
        edge_ref[:, :DEPTH] = (dk[pad : pad + BLOCK] * scale).astype(BF)
        edge_ref[:, DEPTH:] = dv[pad : pad + BLOCK].astype(BF)
        own_ref[:, :DEPTH] = dk[pad + BLOCK :] * scale
        own_ref[:, DEPTH:] = dv[pad + BLOCK :]


def attend(qg, kv, prev, sums, which):
    count = sums.shape[0]
    pad = max(16, -(-count // 16) * 16)
    width = pad + 2 * BLOCK

    def column(col, moving=False):
        if moving:
            return pl.BlockSpec((BLOCK, DEPTH), lambda h: (0, h + col))
        return pl.BlockSpec((BLOCK, DEPTH), lambda h: (0, col))

    def summary(col):
        return pl.BlockSpec((count, sums.shape[1], DEPTH), lambda h: (0, 0, col))

    whole = lambda shape: pl.BlockSpec(shape, lambda h: (0, 0))
    outs = pl.pallas_call(
        attend_kernel,
        grid=(GROUP,),
        in_specs=[
            column(0, True),
            column(GROUP, True),
            column(which),
            column(2 + which),
            column(which),
            column(2 + which),
            summary(which),
            summary(2 + which),
        ],
        out_specs=[
            pl.BlockSpec((BLOCK, DEPTH), lambda h: (0, h)),
            pl.BlockSpec((BLOCK, DEPTH), lambda h: (0, h)),
            whole((BLOCK, 2 * DEPTH)),
            whole((BLOCK, 2 * DEPTH)),
            whole((count, 2 * DEPTH)),
        ],
        out_shape=[
            jax.ShapeDtypeStruct((BLOCK, GROUP * DEPTH), BF),
            jax.ShapeDtypeStruct((BLOCK, GROUP * DEPTH), BF),
            jax.ShapeDtypeStruct((BLOCK, 2 * DEPTH), BF),
            jax.ShapeDtypeStruct((BLOCK, 2 * DEPTH), F32),
            jax.ShapeDtypeStruct((count, 2 * DEPTH), F32),
        ],
        scratch_shapes=[
            pltpu.VMEM((width, DEPTH), BF),
            pltpu.VMEM((width, DEPTH), BF),
            pltpu.VMEM((DEPTH, width), BF),
            pltpu.VMEM((DEPTH, width), BF),
            pltpu.VMEM((width, DEPTH), F32),
            pltpu.VMEM((width, DEPTH), F32),
        ],
        cost_estimate=pl.CostEstimate(
            flops=12 * GROUP * BLOCK * 2 * BLOCK * DEPTH,
            bytes_accessed=8 * BLOCK * GROUP * DEPTH,
            transcendentals=GROUP * BLOCK * 2 * BLOCK,
        ),
        name="attend",
    )(qg, qg, kv, kv, prev, prev, sums, sums)
    return outs


def join_kernel(own_a, own_b, edge_a, edge_b, ds_ref, out_ref):
    total = jnp.sum(ds_ref[...], axis=0, keepdims=True) * (1.0 / BLOCK)
    for g, (own, edge) in enumerate(((own_a, edge_a), (own_b, edge_b))):
        both = own[...] + edge[...].astype(F32)
        for part in range(2):
            cols = slice(part * DEPTH, (part + 1) * DEPTH)
            spread = total[:, (2 * g + part) * DEPTH : (2 * g + part + 1) * DEPTH]
            at = (2 * part + g) * DEPTH
            out_ref[:, at : at + DEPTH] = (both[:, cols] + spread).astype(BF)


def join(own, edge, ds):
    return pl.pallas_call(
        join_kernel,
        out_shape=jax.ShapeDtypeStruct((BLOCK, 4 * DEPTH), BF),
        name="join",
    )(own[0], own[1], edge[0], edge[1], ds)


def unpack_kernel(oa_ref, qa_ref, ob_ref, qb_ref, kv_ref, o_ref, dq_ref, dk_ref, dv_ref):
    half = GROUP * DEPTH
    o_ref[:, :half] = oa_ref[0]
    o_ref[:, half:] = ob_ref[0]
    dq_ref[:, :half] = qa_ref[0]
    dq_ref[:, half:] = qb_ref[0]
    dk_ref[...] = kv_ref[0, :, : 2 * DEPTH]
    dv_ref[...] = kv_ref[0, :, 2 * DEPTH :]


def unpack(oa, qa, ob, qb, kv):
    parts, rows, half = oa.shape
    wide = pl.BlockSpec((1, rows, half), lambda i: (i, 0, 0))
    return pl.pallas_call(
        unpack_kernel,
        grid=(parts,),
        in_specs=[wide, wide, wide, wide, pl.BlockSpec((1, rows, 4 * DEPTH), lambda i: (i, 0, 0))],
        out_specs=[
            pl.BlockSpec((rows, 2 * half), lambda i: (0, i)),
            pl.BlockSpec((rows, 2 * half), lambda i: (0, i)),
            pl.BlockSpec((rows, 2 * DEPTH), lambda i: (0, i)),
            pl.BlockSpec((rows, 2 * DEPTH), lambda i: (0, i)),
        ],
        out_shape=[
            jax.ShapeDtypeStruct((rows, parts * 2 * half), BF),
            jax.ShapeDtypeStruct((rows, parts * 2 * half), BF),
            jax.ShapeDtypeStruct((rows, parts * 2 * DEPTH), BF),
            jax.ShapeDtypeStruct((rows, parts * 2 * DEPTH), BF),
        ],
        name="unpack",
    )(oa, qa, ob, qb, kv)


def exchange(x):
    return lax.all_to_all(x, "head", split_axis=0, concat_axis=0, tiled=True)


def shards(queries, keys, values, cotangent):
    rows = queries.shape[0]
    parts = lax.axis_size("head")
    blocks = lax.axis_size("ctx")
    assert rows * parts == BLOCK and parts * 2 == KEY_VALUE_HEADS
    kv, qg_a, qg_b, sums = pack(queries, keys, values, cotangent, parts)
    kv = exchange(kv).reshape(BLOCK, 4 * DEPTH)
    qg_a = exchange(qg_a).reshape(BLOCK, 2 * GROUP * DEPTH)
    qg_b = exchange(qg_b).reshape(BLOCK, 2 * GROUP * DEPTH)
    prev = lax.ppermute(kv, "ctx", [(i, i + 1) for i in range(blocks - 1)])
    sums = jnp.broadcast_to(sums.reshape(1, parts, 4 * DEPTH), (blocks, parts, 4 * DEPTH))
    sums = lax.all_to_all(
        sums.reshape(blocks * parts, 4 * DEPTH), ("ctx", "head"), 0, 0, tiled=True
    ).reshape(blocks, parts, 4 * DEPTH)
    o_a, q_a, edge_a, own_a, ds_a = attend(qg_a, kv, prev, sums, 0)
    o_b, q_b, edge_b, own_b, ds_b = attend(qg_b, kv, prev, sums, 1)
    back = [(i + 1, i) for i in range(blocks - 1)]
    edge_a = lax.ppermute(edge_a, "ctx", back)
    edge_b = lax.ppermute(edge_b, "ctx", back)
    ds = lax.all_to_all(jnp.concatenate([ds_a, ds_b], axis=1), "ctx", 0, 0, tiled=True)
    split = lambda x: x.reshape(parts, rows, x.shape[1])
    dkv = exchange(split(join((own_a, own_b), (edge_a, edge_b), ds)))
    return tuple(
        unpack(
            exchange(split(o_a)), exchange(split(q_a)),
            exchange(split(o_b)), exchange(split(q_b)), dkv,
        )
    )


def solution(mesh):
    placed = P(("ctx", "head"), None)
    return jax.shard_map(
        shards, mesh=mesh, in_specs=(placed,) * 4, out_specs=(placed,) * 4, check_vma=False
    )
```

```python
import jax
import jax.numpy as jnp
from jax import lax
from jax.experimental import pallas as pl
from jax.experimental.pallas import tpu as pltpu
from jax.sharding import PartitionSpec as P

QUERY_HEADS = 32
KEY_VALUE_HEADS = 8
DEPTH = 128
BLOCK = 512
TILE = 256
GROUP = QUERY_HEADS // KEY_VALUE_HEADS
LOWEST = -1e30
LOG2E = 1.4426950408889634

BF = jnp.bfloat16
F32 = jnp.float32


def dot(a, b, ca, cb):
    return lax.dot_general(a, b, (((ca,), (cb,)), ((), ())), preferred_element_type=F32)


def here(d):
    return lax.axis_index("head") ^ d


def rows_of(d, size):
    return pl.ds(pl.multiple_of(here(d) * size, size), size)


def pack_kv_kernel(k_ref, v_ref, *outs):
    sums_ref = outs[-1]
    blocks = sums_ref.shape[0]
    wide = 2 * DEPTH
    for d, out in enumerate(outs[:-1]):
        cols = rows_of(d, wide)
        out[:, :wide] = k_ref[:, cols]
        out[:, wide:] = v_ref[:, cols]
    for part in range(len(outs) - 1):
        cols = slice(part * wide, (part + 1) * wide)
        ks = jnp.sum(k_ref[:, cols].astype(F32), axis=0, keepdims=True)
        vs = jnp.sum(v_ref[:, cols].astype(F32), axis=0, keepdims=True)
        sums_ref[:, part, :wide] = jnp.broadcast_to(ks, (blocks, wide))
        sums_ref[:, part, wide:] = jnp.broadcast_to(vs, (blocks, wide))


def pack_kv(k, v, parts, blocks):
    rows = k.shape[0]
    outs = pl.pallas_call(
        pack_kv_kernel,
        out_shape=[jax.ShapeDtypeStruct((rows, 4 * DEPTH), BF)] * parts
        + [jax.ShapeDtypeStruct((blocks, parts, 4 * DEPTH), F32)],
        name="pack_kv",
    )(k, v)
    return outs[:-1], outs[-1]


def pack_kernel(*refs):
    parts = len(refs) // 3
    for d in range(parts):
        q_ref, g_ref, out = refs[d], refs[parts + d], refs[2 * parts + d]
        for i in range(GROUP):
            out[i, 0] = q_ref[:, i * DEPTH : (i + 1) * DEPTH]
            out[i, 1] = g_ref[:, i * DEPTH : (i + 1) * DEPTH]


def pack(q, g, which, parts):
    rows = q.shape[0]

    def spec(d):
        return pl.BlockSpec((rows, GROUP * DEPTH), lambda i: (0, 2 * here(d) + which))

    return pl.pallas_call(
        pack_kernel,
        grid=(1,),
        in_specs=[spec(d) for d in range(parts)] * 2,
        out_specs=[pl.BlockSpec((GROUP, 2, rows, DEPTH), lambda i: (0, 0, 0, 0))] * parts,
        out_shape=[jax.ShapeDtypeStruct((GROUP, 2, rows, DEPTH), BF)] * parts,
        name="pack",
    )(*([q] * parts + [g] * parts))


def gather_kernel(*refs):
    a_ref, b_ref = refs[-2:]
    rows = refs[0].shape[0]
    for d, piece in enumerate(refs[:-2]):
        at = rows_of(d, rows)
        for which, out in enumerate((a_ref, b_ref)):
            out[at, :DEPTH] = piece[:, which * DEPTH : (which + 1) * DEPTH]
            out[at, DEPTH:] = piece[:, (2 + which) * DEPTH : (3 + which) * DEPTH]


def gather(pieces):
    return pl.pallas_call(
        gather_kernel,
        out_shape=[jax.ShapeDtypeStruct((BLOCK, 2 * DEPTH), BF)] * 2,
        name="gather_kv",
    )(*pieces)


def attend_kernel(parts, *refs):
    pieces = refs[:parts]
    k_ref, v_ref, pk_ref, pv_ref, sk_ref, sv_ref = refs[parts : parts + 6]
    outs = refs[parts + 6 : 2 * parts + 6]
    edge_ref, own_ref, ds_ref = refs[2 * parts + 6 : 2 * parts + 9]
    kc, vc, kt, vt, dk, dv, qs, gs, os, dqs = refs[2 * parts + 9 :]
    ctx = lax.axis_index("ctx")
    scale = DEPTH ** (-0.5)
    coef = scale * LOG2E
    count = sk_ref.shape[0]
    pad = kc.shape[0] - 2 * BLOCK
    head = pl.program_id(0)
    small = BLOCK // parts

    @pl.when(head == 0)
    def _():
        for ref, all_ref, own, prev, tr in (
            (sk_ref, kc, k_ref, pk_ref, kt),
            (sv_ref, vc, v_ref, pv_ref, vt),
        ):
            mean = (jnp.sum(ref[...], axis=1) * (1.0 / BLOCK)).astype(BF)
            if pad > count:
                mean = jnp.concatenate([mean, jnp.zeros((pad - count, DEPTH), BF)], axis=0)
            all_ref[:pad] = mean
            all_ref[pad : pad + BLOCK] = prev[...]
            all_ref[pad + BLOCK :] = own[...]
            tr[...] = all_ref[...].T
        dk[...] = jnp.zeros_like(dk)
        dv[...] = jnp.zeros_like(dv)

    for d, piece in enumerate(pieces):
        at = rows_of(d, small)
        qs[at, :] = piece[0, 0]
        gs[at, :] = piece[0, 1]

    for tile in range(BLOCK // TILE):
        rows = slice(tile * TILE, (tile + 1) * TILE)
        edge = pad + BLOCK + TILE * (tile + 1)
        q = qs[rows, :]
        s = dot(kc[:edge], q, 1, 1)
        s_sum = s[:pad]
        s_prev = s[pad : pad + BLOCK]
        s_diag = s[edge - TILE :]
        at = lax.broadcasted_iota(jnp.int32, (pad, TILE), 0)
        s_sum = jnp.where(at < ctx, s_sum, LOWEST)
        ki = lax.broadcasted_iota(jnp.int32, (TILE, TILE), 0)
        qi = lax.broadcasted_iota(jnp.int32, (TILE, TILE), 1)
        s_diag = jnp.where(ki <= qi, s_diag, LOWEST)
        slabs = [s_sum, s_prev, s_diag]
        if tile > 0:
            slabs.insert(2, s[pad + BLOCK : edge - TILE])
        tops = [jnp.max(x, axis=0, keepdims=True) for x in slabs]
        tops[1] = jnp.where(ctx > 0, tops[1], LOWEST)
        top = tops[0]
        for x in tops[1:]:
            top = jnp.maximum(top, x)
        shift = [top] * len(slabs)
        shift[1] = jnp.where(ctx > 0, top, -LOWEST)
        weights = [jnp.exp2((x - y) * coef) for x, y in zip(slabs, shift)]
        total = sum(jnp.sum(x, axis=0, keepdims=True) for x in weights)
        inv = 1.0 / total
        weight = jnp.concatenate(weights, axis=0)
        low = weight.astype(BF)
        attended = dot(vt[:, :edge], low, 1, 0) * inv
        os[rows, :] = attended.T.astype(BF)
        gt = (gs[rows, :].astype(F32).T * (16.0 * inv)).astype(BF)
        row_dot = jnp.sum(gt.astype(F32) * attended, axis=0, keepdims=True)
        back = dot(vc[:edge], gt, 1, 0)
        slope = (weight * (back - row_dot)).astype(BF)
        dqs[rows, :] = (dot(kt[:, :edge], slope, 1, 0) * scale).T.astype(BF)
        dk[:edge] += dot(slope, q, 1, 0)
        dv[:edge] += dot(low, gt, 1, 1)

    for d, out in enumerate(outs):
        at = rows_of(d, small)
        out[0, 0] = os[at, :]
        out[0, 1] = dqs[at, :]

    @pl.when(head == pl.num_programs(0) - 1)
    def _():
        ds_ref[:, :DEPTH] = dk[:count] * scale
        ds_ref[:, DEPTH:] = dv[:count]
        edge_ref[:, :DEPTH] = (dk[pad : pad + BLOCK] * scale).astype(BF)
        edge_ref[:, DEPTH:] = dv[pad : pad + BLOCK].astype(BF)
        own_ref[:, :DEPTH] = dk[pad + BLOCK :] * scale
        own_ref[:, DEPTH:] = dv[pad + BLOCK :]


def attend(pieces, kv, prev, sums, which):
    parts = len(pieces)
    small = BLOCK // parts
    count = sums.shape[0]
    pad = max(16, -(-count // 16) * 16)
    width = pad + 2 * BLOCK

    def column(col):
        return pl.BlockSpec((BLOCK, DEPTH), lambda h: (0, col))

    def summary(col):
        return pl.BlockSpec((count, sums.shape[1], DEPTH), lambda h: (0, 0, col))

    piece = pl.BlockSpec((1, 2, small, DEPTH), lambda h: (h, 0, 0, 0))
    whole = lambda shape: pl.BlockSpec(shape, lambda h: (0, 0))
    outs = pl.pallas_call(
        lambda *refs: attend_kernel(parts, *refs),
        grid=(GROUP,),
        in_specs=[piece] * parts
        + [column(0), column(1), column(0), column(1), summary(which), summary(2 + which)],
        out_specs=[piece] * parts
        + [whole((BLOCK, 2 * DEPTH)), whole((BLOCK, 2 * DEPTH)), whole((count, 2 * DEPTH))],
        out_shape=[jax.ShapeDtypeStruct((GROUP, 2, small, DEPTH), BF)] * parts
        + [
            jax.ShapeDtypeStruct((BLOCK, 2 * DEPTH), BF),
            jax.ShapeDtypeStruct((BLOCK, 2 * DEPTH), F32),
            jax.ShapeDtypeStruct((count, 2 * DEPTH), F32),
        ],
        scratch_shapes=[
            pltpu.VMEM((width, DEPTH), BF),
            pltpu.VMEM((width, DEPTH), BF),
            pltpu.VMEM((DEPTH, width), BF),
            pltpu.VMEM((DEPTH, width), BF),
            pltpu.VMEM((width, DEPTH), F32),
            pltpu.VMEM((width, DEPTH), F32),
            pltpu.VMEM((BLOCK, DEPTH), BF),
            pltpu.VMEM((BLOCK, DEPTH), BF),
            pltpu.VMEM((BLOCK, DEPTH), BF),
            pltpu.VMEM((BLOCK, DEPTH), BF),
        ],
        cost_estimate=pl.CostEstimate(
            flops=12 * GROUP * BLOCK * 2 * BLOCK * DEPTH,
            bytes_accessed=8 * BLOCK * GROUP * DEPTH,
            transcendentals=GROUP * BLOCK * 2 * BLOCK,
        ),
        name="attend",
    )(*pieces, kv, kv, prev, prev, sums, sums)
    return outs[:parts], outs[parts], outs[parts + 1], outs[parts + 2]


def join_kernel(own_a, own_b, edge_a, edge_b, *outs):
    rows = outs[0].shape[0]
    for d, out in enumerate(outs):
        at = rows_of(d, rows)
        for g, (own, edge) in enumerate(((own_a, edge_a), (own_b, edge_b))):
            both = (own[at, :] + edge[at, :].astype(F32)).astype(BF)
            out[:, g * DEPTH : (g + 1) * DEPTH] = both[:, :DEPTH]
            out[:, (2 + g) * DEPTH : (3 + g) * DEPTH] = both[:, DEPTH:]


def join(own, edge, parts):
    return pl.pallas_call(
        join_kernel,
        out_shape=[jax.ShapeDtypeStruct((BLOCK // parts, 4 * DEPTH), BF)] * parts,
        name="join",
    )(own[0], own[1], edge[0], edge[1])


def unpack_kernel(*refs):
    parts = (len(refs) - 2) // 2
    o_ref, dq_ref = refs[-2:]
    for g in range(2):
        for d in range(parts):
            piece = refs[g * parts + d]
            for i in range(GROUP):
                at = pl.ds(pl.multiple_of(((2 * here(d) + g) * GROUP + i) * DEPTH, DEPTH), DEPTH)
                o_ref[:, at] = piece[i, 0]
                dq_ref[:, at] = piece[i, 1]


def unpack(a, b):
    parts = len(a)
    rows = a[0].shape[2]
    shape = jax.ShapeDtypeStruct((rows, parts * 2 * GROUP * DEPTH), BF)
    return pl.pallas_call(unpack_kernel, out_shape=[shape, shape], name="unpack")(*a, *b)


def finish(pieces, ds):
    parts = len(pieces)
    rows = pieces[0].shape[0]
    wide = 2 * DEPTH

    def kernel(*refs):
        ds_ref, dk_ref, dv_ref, tot = refs[parts:]
        tot[...] = jnp.sum(ds_ref[...], axis=0) * (1.0 / BLOCK)
        for d in range(parts):
            at = rows_of(d, wide)
            spread = tot[pl.ds(here(d), 1), :]
            full = (refs[d][...].astype(F32) + spread).astype(BF)
            dk_ref[:, at] = full[:, :wide]
            dv_ref[:, at] = full[:, wide:]

    shape = jax.ShapeDtypeStruct((rows, parts * wide), BF)
    return pl.pallas_call(
        kernel,
        out_shape=[shape, shape],
        scratch_shapes=[pltpu.VMEM((parts, 2 * wide), F32)],
        name="finish",
    )(*pieces, ds)


def swap(pieces):
    parts = len(pieces)
    moved = [
        lax.ppermute(pieces[d], "head", [(i, i ^ d) for i in range(parts)]) for d in range(1, parts)
    ]
    return [pieces[0]] + moved


def shards(queries, keys, values, cotangent):
    rows = queries.shape[0]
    parts = lax.axis_size("head")
    blocks = lax.axis_size("ctx")
    assert rows * parts == BLOCK and parts * 2 == KEY_VALUE_HEADS
    forth = [(i, i + 1) for i in range(blocks - 1)]
    back = [(i + 1, i) for i in range(blocks - 1)]
    kv, sums = pack_kv(keys, values, parts, blocks)
    kv = swap(kv)
    pieces_a = swap(pack(queries, cotangent, 0, parts))
    pieces_b = swap(pack(queries, cotangent, 1, parts))
    kv_a, kv_b = gather(kv)
    prev_a = lax.ppermute(kv_a, "ctx", forth)
    prev_b = lax.ppermute(kv_b, "ctx", forth)
    sums = lax.all_to_all(
        sums.reshape(blocks * parts, 4 * DEPTH), ("ctx", "head"), 0, 0, tiled=True
    ).reshape(blocks, parts, 4 * DEPTH)
    out_a, edge_a, own_a, ds_a = attend(pieces_a, kv_a, prev_a, sums, 0)
    out_a = swap(out_a)
    edge_a = lax.ppermute(edge_a, "ctx", back)
    out_b, edge_b, own_b, ds_b = attend(pieces_b, kv_b, prev_b, sums, 1)
    edge_b = lax.ppermute(edge_b, "ctx", back)
    out_b = swap(out_b)
    ds = jnp.concatenate(
        [ds_a[:, :DEPTH], ds_b[:, :DEPTH], ds_a[:, DEPTH:], ds_b[:, DEPTH:]], axis=1
    )
    ds = jnp.broadcast_to(ds[:, None], (blocks, parts, 4 * DEPTH))
    ds = lax.all_to_all(
        ds.reshape(blocks * parts, 4 * DEPTH), ("ctx", "head"), 0, 0, tiled=True
    ).reshape(blocks, parts, 4 * DEPTH)
    dkv = swap(join((own_a, own_b), (edge_a, edge_b), parts))
    out, grad_queries = unpack(out_a, out_b)
    grad_keys, grad_values = finish(dkv, ds)
    return out, grad_queries, grad_keys, grad_values


def solution(mesh):
    placed = P(("ctx", "head"), None)
    return jax.shard_map(
        shards, mesh=mesh, in_specs=(placed,) * 4, out_specs=(placed,) * 4, check_vma=False
    )
```

```python
import jax
import jax.numpy as jnp
from jax import lax
from jax.experimental import pallas as pl
from jax.experimental.pallas import tpu as pltpu
from jax.sharding import PartitionSpec as P


QUERY_HEADS = 32
KEY_VALUE_HEADS = 8
DEPTH = 128
BLOCK = 512
TILE = 256
GROUP = QUERY_HEADS // KEY_VALUE_HEADS
LOWEST = -1e30
LOG2E = 1.4426950408889634

BF = jnp.bfloat16
F32 = jnp.float32


def dot(a, b, ca, cb):
    return lax.dot_general(a, b, (((ca,), (cb,)), ((), ())), preferred_element_type=F32)


VM = pl.BlockSpec(memory_space=pltpu.VMEM)
ROOM = pltpu.CompilerParams(vmem_limit_bytes=12 << 20)


def here(d):
    return lax.axis_index("head") ^ d


def rows_of(d, size):
    return pl.ds(pl.multiple_of(here(d) * size, size), size)


def pack_kv_kernel(k_ref, v_ref, *outs):
    sums_ref = outs[-1]
    blocks = sums_ref.shape[0]
    wide = 2 * DEPTH
    for d, out in enumerate(outs[:-1]):
        cols = rows_of(d, wide)
        out[:, :wide] = k_ref[:, cols]
        out[:, wide:] = v_ref[:, cols]
    for part in range(len(outs) - 1):
        cols = slice(part * wide, (part + 1) * wide)
        ks = jnp.sum(k_ref[:, cols].astype(F32), axis=0, keepdims=True)
        vs = jnp.sum(v_ref[:, cols].astype(F32), axis=0, keepdims=True)
        sums_ref[:, part, :wide] = jnp.broadcast_to(ks, (blocks, wide))
        sums_ref[:, part, wide:] = jnp.broadcast_to(vs, (blocks, wide))


def pack_kv(k, v, parts, blocks):
    rows = k.shape[0]
    outs = pl.pallas_call(
        pack_kv_kernel,
        out_shape=[jax.ShapeDtypeStruct((rows, 4 * DEPTH), BF)] * parts
        + [jax.ShapeDtypeStruct((blocks, parts, 4 * DEPTH), F32)],
        out_specs=[VM] * (parts + 1),
        compiler_params=ROOM, name="pack_kv",
    )(k, v)
    return outs[:-1], outs[-1]


def pack_kernel(*refs):
    parts = len(refs) // 3
    for d in range(parts):
        q_ref, g_ref, out = refs[d], refs[parts + d], refs[2 * parts + d]
        for i in range(GROUP):
            out[i, 0] = q_ref[:, i * DEPTH : (i + 1) * DEPTH]
            out[i, 1] = g_ref[:, i * DEPTH : (i + 1) * DEPTH]


def pack(q, g, which, parts):
    rows = q.shape[0]

    def spec(d):
        return pl.BlockSpec((rows, GROUP * DEPTH), lambda i: (0, 2 * here(d) + which))

    return pl.pallas_call(
        pack_kernel,
        grid=(1,),
        in_specs=[spec(d) for d in range(parts)] * 2,
        out_specs=[VM] * parts,
        out_shape=[jax.ShapeDtypeStruct((GROUP, 2, rows, DEPTH), BF)] * parts,
        compiler_params=ROOM, name="pack",
    )(*([q] * parts + [g] * parts))


def gather_kernel(*refs):
    a_ref, b_ref = refs[-2:]
    rows = refs[0].shape[0]
    for d, piece in enumerate(refs[:-2]):
        at = rows_of(d, rows)
        for which, out in enumerate((a_ref, b_ref)):
            out[at, :DEPTH] = piece[:, which * DEPTH : (which + 1) * DEPTH]
            out[at, DEPTH:] = piece[:, (2 + which) * DEPTH : (3 + which) * DEPTH]


def gather(pieces):
    return pl.pallas_call(
        gather_kernel,
        in_specs=[VM] * len(pieces),
        out_specs=[VM] * 2,
        out_shape=[jax.ShapeDtypeStruct((BLOCK, 2 * DEPTH), BF)] * 2,
        compiler_params=ROOM, name="gather_kv",
    )(*pieces)


def attend_kernel(parts, which, *refs):
    pieces = refs[:parts]
    kv_ref, prev_ref, sums_ref = refs[parts : parts + 3]
    outs = refs[parts + 3 : 2 * parts + 3]
    edge_ref, own_ref, ds_ref = refs[2 * parts + 3 : 2 * parts + 6]
    kc, vc, kt, vt, dk, dv, qs, gs, os, dqs = refs[2 * parts + 6 :]
    ctx = lax.axis_index("ctx")
    scale = DEPTH ** (-0.5)
    coef = scale * LOG2E
    count = sums_ref.shape[0]
    pad = kc.shape[0] - 2 * BLOCK
    small = BLOCK // parts

    mean = (jnp.sum(sums_ref[...], axis=1) * (1.0 / BLOCK)).astype(BF)
    if pad > count:
        mean = jnp.concatenate([mean, jnp.zeros((pad - count, 4 * DEPTH), BF)], axis=0)
    for part, (all_ref, tr) in enumerate(((kc, kt), (vc, vt))):
        cols = slice(part * DEPTH, (part + 1) * DEPTH)
        at = (2 * part + which) * DEPTH
        all_ref[:pad] = mean[:, at : at + DEPTH]
        all_ref[pad : pad + BLOCK] = prev_ref[:, cols]
        all_ref[pad + BLOCK :] = kv_ref[:, cols]
        tr[...] = all_ref[...].T
    dk[...] = jnp.zeros_like(dk)
    dv[...] = jnp.zeros_like(dv)

    def step(head, carry):
        for d, piece in enumerate(pieces):
            at = rows_of(d, small)
            qs[at, :] = piece[head, 0]
            gs[at, :] = piece[head, 1]

        for tile in range(BLOCK // TILE):
            rows = slice(tile * TILE, (tile + 1) * TILE)
            edge = pad + BLOCK + TILE * (tile + 1)
            q = qs[rows, :]
            s = dot(kc[:edge], q, 1, 1)
            s_sum = s[:pad]
            s_prev = s[pad : pad + BLOCK]
            s_diag = s[edge - TILE :]
            at = lax.broadcasted_iota(jnp.int32, (pad, TILE), 0)
            s_sum = jnp.where(at < ctx, s_sum, LOWEST)
            ki = lax.broadcasted_iota(jnp.int32, (TILE, TILE), 0)
            qi = lax.broadcasted_iota(jnp.int32, (TILE, TILE), 1)
            s_diag = jnp.where(ki <= qi, s_diag, LOWEST)
            slabs = [s_sum, s_prev, s_diag]
            if tile > 0:
                slabs.insert(2, s[pad + BLOCK : edge - TILE])
            tops = [jnp.max(x, axis=0, keepdims=True) for x in slabs]
            tops[1] = jnp.where(ctx > 0, tops[1], LOWEST)
            top = tops[0]
            for x in tops[1:]:
                top = jnp.maximum(top, x)
            shift = [top] * len(slabs)
            shift[1] = jnp.where(ctx > 0, top, -LOWEST)
            weights = [jnp.exp2((x - y) * coef) for x, y in zip(slabs, shift)]
            total = sum(jnp.sum(x, axis=0, keepdims=True) for x in weights)
            inv = 1.0 / total
            weight = jnp.concatenate(weights, axis=0)
            low = weight.astype(BF)
            attended = dot(vt[:, :edge], low, 1, 0) * inv
            os[rows, :] = attended.T.astype(BF)
            gt = (gs[rows, :].astype(F32).T * (16.0 * inv)).astype(BF)
            row_dot = jnp.sum(gt.astype(F32) * attended, axis=0, keepdims=True)
            back = dot(vc[:edge], gt, 1, 0)
            slope = (weight * (back - row_dot)).astype(BF)
            dqs[rows, :] = (dot(kt[:, :edge], slope, 1, 0) * scale).T.astype(BF)
            dk[:edge] += dot(slope, q, 1, 0)
            dv[:edge] += dot(low, gt, 1, 1)

        for d, out in enumerate(outs):
            at = rows_of(d, small)
            out[head, 0] = os[at, :]
            out[head, 1] = dqs[at, :]
        return carry

    lax.fori_loop(0, GROUP, step, 0)
    ds_ref[:, :DEPTH] = dk[:count] * scale
    ds_ref[:, DEPTH:] = dv[:count]
    edge_ref[:, :DEPTH] = (dk[pad : pad + BLOCK] * scale).astype(BF)
    edge_ref[:, DEPTH:] = dv[pad : pad + BLOCK].astype(BF)
    own_ref[:, :DEPTH] = dk[pad + BLOCK :] * scale
    own_ref[:, DEPTH:] = dv[pad + BLOCK :]


def attend(pieces, kv, prev, sums, which):
    parts = len(pieces)
    small = BLOCK // parts
    count = sums.shape[0]
    pad = max(16, -(-count // 16) * 16)
    width = pad + 2 * BLOCK
    outs = pl.pallas_call(
        lambda *refs: attend_kernel(parts, which, *refs),
        in_specs=[VM] * (parts + 3),
        out_specs=[VM] * (parts + 3),
        out_shape=[jax.ShapeDtypeStruct((GROUP, 2, small, DEPTH), BF)] * parts
        + [
            jax.ShapeDtypeStruct((BLOCK, 2 * DEPTH), BF),
            jax.ShapeDtypeStruct((BLOCK, 2 * DEPTH), F32),
            jax.ShapeDtypeStruct((count, 2 * DEPTH), F32),
        ],
        scratch_shapes=[
            pltpu.VMEM((width, DEPTH), BF),
            pltpu.VMEM((width, DEPTH), BF),
            pltpu.VMEM((DEPTH, width), BF),
            pltpu.VMEM((DEPTH, width), BF),
            pltpu.VMEM((width, DEPTH), F32),
            pltpu.VMEM((width, DEPTH), F32),
            pltpu.VMEM((BLOCK, DEPTH), BF),
            pltpu.VMEM((BLOCK, DEPTH), BF),
            pltpu.VMEM((BLOCK, DEPTH), BF),
            pltpu.VMEM((BLOCK, DEPTH), BF),
        ],
        compiler_params=pltpu.CompilerParams(vmem_limit_bytes=24 << 20),
        cost_estimate=pl.CostEstimate(
            flops=12 * GROUP * BLOCK * 2 * BLOCK * DEPTH,
            bytes_accessed=8 * BLOCK * GROUP * DEPTH,
            transcendentals=GROUP * BLOCK * 2 * BLOCK,
        ),
        name="attend",
    )(*pieces, kv, prev, sums)
    return outs[:parts], outs[parts], outs[parts + 1], outs[parts + 2]


def join_kernel(own_a, own_b, edge_a, edge_b, ds_ref, *outs):
    rows = outs[0].shape[0]
    total = jnp.sum(ds_ref[...], axis=0, keepdims=True) * (1.0 / BLOCK)
    for d, out in enumerate(outs):
        at = rows_of(d, rows)
        for g, (own, edge) in enumerate(((own_a, edge_a), (own_b, edge_b))):
            both = own[at, :] + edge[at, :].astype(F32)
            both = (both + total[:, 2 * g * DEPTH : 2 * (g + 1) * DEPTH]).astype(BF)
            out[:, g * DEPTH : (g + 1) * DEPTH] = both[:, :DEPTH]
            out[:, (2 + g) * DEPTH : (3 + g) * DEPTH] = both[:, DEPTH:]


def join(own, edge, ds, parts):
    return pl.pallas_call(
        join_kernel,
        in_specs=[VM] * 5,
        out_specs=[VM] * parts,
        out_shape=[jax.ShapeDtypeStruct((BLOCK // parts, 4 * DEPTH), BF)] * parts,
        compiler_params=ROOM, name="join",
    )(own[0], own[1], edge[0], edge[1], ds)


def unpack_kernel(*refs):
    parts = (len(refs) - 2) // 2
    o_ref, dq_ref = refs[-2:]
    for g in range(2):
        for d in range(parts):
            piece = refs[g * parts + d]
            for i in range(GROUP):
                at = pl.ds(pl.multiple_of(((2 * here(d) + g) * GROUP + i) * DEPTH, DEPTH), DEPTH)
                o_ref[:, at] = piece[i, 0]
                dq_ref[:, at] = piece[i, 1]


def unpack(a, b):
    parts = len(a)
    rows = a[0].shape[2]
    shape = jax.ShapeDtypeStruct((rows, parts * 2 * GROUP * DEPTH), BF)
    return pl.pallas_call(unpack_kernel, in_specs=[VM] * (2 * parts), out_shape=[shape, shape], compiler_params=ROOM, name="unpack")(*a, *b)


def finish_kernel(*refs):
    parts = len(refs) - 2
    dk_ref, dv_ref = refs[-2:]
    wide = 2 * DEPTH
    for d in range(parts):
        at = rows_of(d, wide)
        dk_ref[:, at] = refs[d][:, :wide]
        dv_ref[:, at] = refs[d][:, wide:]


def finish(pieces):
    parts = len(pieces)
    shape = jax.ShapeDtypeStruct((pieces[0].shape[0], parts * 2 * DEPTH), BF)
    return pl.pallas_call(
        finish_kernel, in_specs=[VM] * parts, out_shape=[shape, shape], compiler_params=ROOM, name="finish"
    )(*pieces)


def swap(pieces):
    parts = len(pieces)
    moved = []
    for d in range(1, parts):
        pairs = [(i, i ^ d) for i in range(parts)]
        moved.append(lax.ppermute(pieces[d], "head", pairs))
    return [pieces[0]] + moved


def layer(queries, keys, values, cotangent):
    rows = queries.shape[0]
    parts = lax.axis_size("head")
    blocks = lax.axis_size("ctx")
    assert rows * parts == BLOCK and parts * 2 == KEY_VALUE_HEADS
    forth = [(i, i + 1) for i in range(blocks - 1)]
    back = [(i + 1, i) for i in range(blocks - 1)]
    kv, sums = pack_kv(keys, values, parts, blocks)
    kv = swap(kv)
    pieces_a = pack(queries, cotangent, 0, parts)
    pieces_a = swap(pieces_a)
    pieces_b = pack(queries, cotangent, 1, parts)
    pieces_b = swap(pieces_b)
    kv_a, kv_b = gather(kv)
    prev_a = lax.ppermute(kv_a, "ctx", forth)
    prev_b = lax.ppermute(kv_b, "ctx", forth)
    sums = lax.all_to_all(
        sums.reshape(blocks * parts, 4 * DEPTH), ("ctx", "head"), 0, 0, tiled=True
    ).reshape(blocks, parts, 4 * DEPTH)
    out_a, edge_a, own_a, ds_a = attend(pieces_a, kv_a, prev_a, sums, 0)
    out_a = swap(out_a)
    edge_a = lax.ppermute(edge_a, "ctx", back)
    out_b, edge_b, own_b, ds_b = attend(pieces_b, kv_b, prev_b, sums, 1)
    edge_b = lax.ppermute(edge_b, "ctx", back)
    out_b = swap(out_b)
    ds = jnp.concatenate([ds_a, ds_b], axis=1)
    ds = lax.all_to_all(ds, "ctx", 0, 0, tiled=True)
    dkv = join((own_a, own_b), (edge_a, edge_b), ds, parts)
    dkv = swap(dkv)
    out, grad_queries = unpack(out_a, out_b)
    grad_keys, grad_values = finish(dkv)
    return out, grad_queries, grad_keys, grad_values


def solution(mesh):
    placed = P(("ctx", "head"), None)
    return jax.shard_map(
        layer, mesh=mesh, in_specs=(placed,) * 4, out_specs=(placed,) * 4, check_vma=False
    )
```

```python
import jax
import jax.numpy as jnp
from jax import lax
from jax.experimental import pallas as pl
from jax.experimental.pallas import tpu as pltpu
from jax.sharding import PartitionSpec as P


QUERY_HEADS = 32
KEY_VALUE_HEADS = 8
DEPTH = 128
BLOCK = 512
TILE = 256
GROUP = QUERY_HEADS // KEY_VALUE_HEADS
LOWEST = -1e30
LOG2E = 1.4426950408889634

BF = jnp.bfloat16
F32 = jnp.float32


def dot(a, b, ca, cb):
    return lax.dot_general(a, b, (((ca,), (cb,)), ((), ())), preferred_element_type=F32)


VM = pl.BlockSpec(memory_space=pltpu.VMEM)
HB = pl.BlockSpec(memory_space=pltpu.HBM)
ROOM = pltpu.CompilerParams(vmem_limit_bytes=12 << 20)


def here(d):
    return lax.axis_index("head") ^ d


def rows_of(d, size):
    return pl.ds(pl.multiple_of(here(d) * size, size), size)


def run(copies):
    for copy in copies:
        copy.start()
    for copy in copies:
        copy.wait()


def cols_of(start, size):
    return pl.ds(pl.multiple_of(start * size, size), size)


def pack_kv_kernel(k_ref, v_ref, *outs):
    sems, outs = outs[-1], outs[:-1]
    wide = 2 * DEPTH
    copies = []
    for d, out in enumerate(outs):
        cols = cols_of(here(d), wide)
        for i, ref in enumerate((k_ref, v_ref)):
            half = out.at[:, pl.ds(i * wide, wide)]
            copies.append(pltpu.make_async_copy(ref.at[:, cols], half, sems.at[2 * d + i]))
    run(copies)


def pack_kv(k, v, parts):
    rows = k.shape[0]
    return pl.pallas_call(
        pack_kv_kernel,
        in_specs=[HB] * 2,
        out_specs=[VM] * parts,
        out_shape=[jax.ShapeDtypeStruct((rows, 4 * DEPTH), BF)] * parts,
        scratch_shapes=[pltpu.SemaphoreType.DMA((2 * parts,))],
        compiler_params=ROOM,
        name="pack_kv",
    )(k, v)


def pack_kernel(q_ref, g_ref, *outs):
    sems, outs = outs[-1], outs[:-1]
    parts = len(outs) // 2
    copies = []
    for which in range(2):
        for d in range(parts):
            cols = cols_of(2 * here(d) + which, GROUP * DEPTH)
            for i, ref in enumerate((q_ref, g_ref)):
                out = outs[which * parts + d].at[i]
                copies.append(pltpu.make_async_copy(ref.at[:, cols], out, sems.at[len(copies)]))
    run(copies)


def pack(q, g, parts):
    outs = pl.pallas_call(
        pack_kernel,
        in_specs=[HB] * 2,
        out_specs=[VM] * (2 * parts),
        out_shape=[jax.ShapeDtypeStruct((2, q.shape[0], GROUP * DEPTH), BF)] * (2 * parts),
        scratch_shapes=[pltpu.SemaphoreType.DMA((4 * parts,))],
        compiler_params=ROOM,
        name="pack",
    )(q, g)
    return outs[:parts], outs[parts:]


def gather_kernel(*refs):
    a_ref, b_ref, sums_ref = refs[-3:]
    rows = refs[0].shape[0]
    total = jnp.zeros((1, 4 * DEPTH), F32)
    for d, piece in enumerate(refs[:-3]):
        at = rows_of(d, rows)
        for which, out in enumerate((a_ref, b_ref)):
            out[at, :DEPTH] = piece[:, which * DEPTH : (which + 1) * DEPTH]
            out[at, DEPTH:] = piece[:, (2 + which) * DEPTH : (3 + which) * DEPTH]
        total = total + jnp.sum(piece[...].astype(F32), axis=0, keepdims=True)
    for block in range(sums_ref.shape[0]):
        sums_ref[block] = total


def gather(pieces, blocks):
    return pl.pallas_call(
        gather_kernel,
        in_specs=[VM] * len(pieces),
        out_specs=[VM] * 3,
        out_shape=[jax.ShapeDtypeStruct((BLOCK, 2 * DEPTH), BF)] * 2
        + [jax.ShapeDtypeStruct((blocks, 1, 4 * DEPTH), F32)],
        compiler_params=ROOM,
        name="gather_kv",
    )(*pieces)


def unflatten(refs):
    return (*refs[:10], refs[10:12], refs[12:14], refs[14], refs[15])


def attend_kernel(parts, which, *refs):
    pieces = refs[:parts]
    kv_ref, prev_ref, sums_ref = refs[parts : parts + 3]
    outs = refs[parts + 3 : 2 * parts + 3]
    edge_ref, own_ref, ds_ref = refs[2 * parts + 3 : 2 * parts + 6]
    kc, vc, kt, vt, dk, dv, qs, gs, os, dqs, sbufs, lbufs, dbuf, tops = unflatten(refs[2 * parts + 6 :])
    ctx = lax.axis_index("ctx")
    scale = DEPTH ** (-0.5)
    coef = scale * LOG2E
    count = sums_ref.shape[0]
    pad = kc.shape[0] - 2 * BLOCK
    small = BLOCK // parts

    mean = jnp.concatenate([sums_ref[c] for c in range(count)], axis=0)
    mean = (mean * (1.0 / BLOCK)).astype(BF)
    if pad > count:
        mean = jnp.concatenate([mean, jnp.zeros((pad - count, 4 * DEPTH), BF)], axis=0)
    for part, (all_ref, tr) in enumerate(((kc, kt), (vc, vt))):
        cols = slice(part * DEPTH, (part + 1) * DEPTH)
        at = (2 * part + which) * DEPTH
        all_ref[:pad] = mean[:, at : at + DEPTH]
        all_ref[pad : pad + BLOCK] = prev_ref[:, cols]
        all_ref[pad + BLOCK :] = kv_ref[:, cols]
        tr[...] = all_ref[...].T
    dk[...] = jnp.zeros_like(dk)
    dv[...] = jnp.zeros_like(dv)

    def extent(tile):
        return pad + BLOCK + TILE * (tile + 1)

    def chunks(tile):
        cuts = [0] + list(range(pad + TILE, extent(tile) + 1, TILE))
        return list(zip(cuts[:-1], cuts[1:]))

    def fetch(head):
        for d, piece in enumerate(pieces):
            at = rows_of(d, small)
            qs[at, :] = piece[0, :, cols_of(head, DEPTH)]
            gs[at, :] = piece[1, :, cols_of(head, DEPTH)]

    def rows_in(tile):
        return slice(tile * TILE, (tile + 1) * TILE)

    def scores(tile):
        state = dict(own=jnp.full((1, TILE), LOWEST, F32), prev=jnp.full((1, TILE), LOWEST, F32))

        def part(lo, hi):
            def go():
                s = dot(kc[lo:hi], qs[rows_in(tile), :], 1, 1)
                if lo == 0:
                    at = lax.broadcasted_iota(jnp.int32, (pad, TILE), 0)
                    first = jnp.where(at < ctx, s[:pad], LOWEST)
                    sbufs[tile][:pad] = first
                    state["own"] = jnp.maximum(state["own"], jnp.max(first, axis=0, keepdims=True))
                    s = s[pad:]
                if hi == extent(tile):
                    ki = lax.broadcasted_iota(jnp.int32, (TILE, TILE), 0)
                    qi = lax.broadcasted_iota(jnp.int32, (TILE, TILE), 1)
                    s = jnp.where(ki <= qi, s, LOWEST)
                sbufs[tile][max(lo, pad) : hi] = s
                name = "prev" if hi <= pad + BLOCK else "own"
                state[name] = jnp.maximum(state[name], jnp.max(s, axis=0, keepdims=True))
                if hi == extent(tile):
                    prev = jnp.where(ctx > 0, state["prev"], LOWEST)
                    tops[tile] = jnp.maximum(state["own"], prev)

            return go

        return [part(lo, hi) for lo, hi in chunks(tile)]

    def weigh(tile, state):
        def part(lo, hi):
            def go():
                top = tops[tile]
                behind = jnp.where(ctx > 0, top, -LOWEST)
                edges = [(lo, pad, top), (pad, hi, behind)] if lo == 0 else [
                    (lo, hi, behind if hi <= pad + BLOCK else top)
                ]
                for a, b, shift in edges:
                    w = jnp.exp2((sbufs[tile][a:b] - shift) * coef)
                    sbufs[tile][a:b] = w
                    lbufs[tile][a:b] = w.astype(BF)
                    total = jnp.sum(w, axis=0, keepdims=True)
                    state["total"] = total + state["total"] if "total" in state else total

            return go

        return [part(lo, hi) for lo, hi in chunks(tile)]

    def gradients(tile, state):
        edge = extent(tile)
        rows = rows_in(tile)

        def out():
            inv = 1.0 / state["total"]
            attended = dot(vt[:, :edge], lbufs[tile][:edge], 1, 0) * inv
            os[rows, :] = attended.T.astype(BF)
            gt = (gs[rows, :].astype(F32).T * (16.0 * inv)).astype(BF)
            state["gt"] = gt
            state["dot"] = jnp.sum(gt.astype(F32) * attended, axis=0, keepdims=True)

        def part(lo, hi):
            def go():
                back = dot(vc[lo:hi], state["gt"], 1, 0)
                dbuf[lo:hi] = (sbufs[tile][lo:hi] * (back - state["dot"])).astype(BF)

            return go

        def query():
            dqs[rows, :] = (dot(kt[:, :edge], dbuf[:edge], 1, 0) * scale).T.astype(BF)

        def store(lo, hi):
            def go():
                dv[lo:hi] += dot(lbufs[tile][lo:hi], state["gt"], 1, 1)
                dk[lo:hi] += dot(dbuf[lo:hi], qs[rows, :], 1, 0)

            return go

        steps = [out] + [part(lo, hi) for lo, hi in chunks(tile)] + [query]
        return steps + [store(lo, hi) for lo, hi in chunks(tile)]

    def weave(*stages):
        order = []
        for n, stage in enumerate(stages):
            order += [((i + 0.5) / len(stage), n, i, go) for i, go in enumerate(stage)]
        for item in sorted(order, key=lambda x: x[:3]):
            item[3]()

    fetch(0)
    weave(scores(0))

    def step(head, carry):
        first, second = {}, {}
        weave(scores(1), weigh(0, first))
        weave(gradients(0, first), weigh(1, second))
        weave(gradients(1, second))
        for d, out in enumerate(outs):
            at = rows_of(d, small)
            out[0, :, cols_of(head, DEPTH)] = os[at, :]
            out[1, :, cols_of(head, DEPTH)] = dqs[at, :]
        fetch(jnp.minimum(head + 1, GROUP - 1))
        weave(scores(0))
        return carry

    lax.fori_loop(0, GROUP, step, 0)
    ds_ref[:, :DEPTH] = dk[:count] * scale
    ds_ref[:, DEPTH:] = dv[:count]
    edge_ref[:, :DEPTH] = (dk[pad : pad + BLOCK] * scale).astype(BF)
    edge_ref[:, DEPTH:] = dv[pad : pad + BLOCK].astype(BF)
    own_ref[:, :DEPTH] = dk[pad + BLOCK :] * scale
    own_ref[:, DEPTH:] = dv[pad + BLOCK :]


def attend(pieces, kv, prev, sums, which):
    parts = len(pieces)
    small = BLOCK // parts
    count = sums.shape[0]
    pad = max(16, -(-count // 16) * 16)
    width = pad + 2 * BLOCK
    outs = pl.pallas_call(
        lambda *refs: attend_kernel(parts, which, *refs),
        in_specs=[VM] * (parts + 3),
        out_specs=[VM] * (parts + 3),
        out_shape=[jax.ShapeDtypeStruct((2, small, GROUP * DEPTH), BF)] * parts
        + [
            jax.ShapeDtypeStruct((BLOCK, 2 * DEPTH), BF),
            jax.ShapeDtypeStruct((BLOCK, 2 * DEPTH), F32),
            jax.ShapeDtypeStruct((count, 2 * DEPTH), F32),
        ],
        scratch_shapes=[
            pltpu.VMEM((width, DEPTH), BF),
            pltpu.VMEM((width, DEPTH), BF),
            pltpu.VMEM((DEPTH, width), BF),
            pltpu.VMEM((DEPTH, width), BF),
            pltpu.VMEM((width, DEPTH), F32),
            pltpu.VMEM((width, DEPTH), F32),
            pltpu.VMEM((BLOCK, DEPTH), BF),
            pltpu.VMEM((BLOCK, DEPTH), BF),
            pltpu.VMEM((BLOCK, DEPTH), BF),
            pltpu.VMEM((BLOCK, DEPTH), BF),
            pltpu.VMEM((width - TILE, TILE), F32),
            pltpu.VMEM((width, TILE), F32),
            pltpu.VMEM((width - TILE, TILE), BF),
            pltpu.VMEM((width, TILE), BF),
            pltpu.VMEM((width, TILE), BF),
            pltpu.VMEM((2, 1, TILE), F32),
        ],
        compiler_params=pltpu.CompilerParams(vmem_limit_bytes=24 << 20),
        cost_estimate=pl.CostEstimate(
            flops=12 * GROUP * BLOCK * 2 * BLOCK * DEPTH,
            bytes_accessed=8 * BLOCK * GROUP * DEPTH,
            transcendentals=GROUP * BLOCK * 2 * BLOCK,
        ),
        name="attend",
    )(*pieces, kv, prev, sums)
    return outs[:parts], outs[parts], outs[parts + 1], outs[parts + 2]


def join_kernel(own_a, own_b, edge_a, edge_b, *outs):
    rows = outs[0].shape[0]
    for d, out in enumerate(outs):
        at = rows_of(d, rows)
        for g, (own, edge) in enumerate(((own_a, edge_a), (own_b, edge_b))):
            both = (own[at, :] + edge[at, :].astype(F32)).astype(BF)
            out[:, g * DEPTH : (g + 1) * DEPTH] = both[:, :DEPTH]
            out[:, (2 + g) * DEPTH : (3 + g) * DEPTH] = both[:, DEPTH:]


def join(own, edge, parts):
    return pl.pallas_call(
        join_kernel,
        in_specs=[VM] * 4,
        out_specs=[VM] * parts,
        out_shape=[jax.ShapeDtypeStruct((BLOCK // parts, 4 * DEPTH), BF)] * parts,
        compiler_params=ROOM,
        name="join",
    )(own[0], own[1], edge[0], edge[1])


def spread_kernel(a_ref, b_ref, out_ref):
    blocks = a_ref.shape[0]
    parts = out_ref.shape[0] // blocks
    for block in range(blocks):
        for g, ref in enumerate((a_ref, b_ref)):
            row = ref[block : block + 1, :]
            for i in range(2):
                at = (2 * i + g) * DEPTH
                part = row[:, i * DEPTH : (i + 1) * DEPTH]
                for h in range(parts):
                    out_ref[block * parts + h, :, at : at + DEPTH] = part


def spread(a, b, parts):
    return pl.pallas_call(
        spread_kernel,
        in_specs=[VM] * 2,
        out_specs=VM,
        out_shape=jax.ShapeDtypeStruct((a.shape[0] * parts, 1, 4 * DEPTH), F32),
        compiler_params=ROOM,
        name="spread",
    )(a, b)


def unpack_kernel(*refs):
    sems, outs, pieces = refs[-1], refs[-3:-1], refs[:-3]
    parts = len(pieces) // 2
    copies = []
    for n, piece in enumerate(pieces):
        cols = cols_of(2 * here(n % parts) + n // parts, GROUP * DEPTH)
        for i, out in enumerate(outs):
            copies.append(
                pltpu.make_async_copy(piece.at[i], out.at[:, cols], sems.at[len(copies)])
            )
    run(copies)


def unpack(a, b):
    parts = len(a)
    rows = a[0].shape[1]
    shape = jax.ShapeDtypeStruct((rows, parts * 2 * GROUP * DEPTH), BF)
    return pl.pallas_call(
        unpack_kernel,
        in_specs=[VM] * (2 * parts),
        out_specs=[HB] * 2,
        out_shape=[shape, shape],
        scratch_shapes=[pltpu.SemaphoreType.DMA((4 * parts,))],
        compiler_params=ROOM,
        name="unpack",
    )(*a, *b)


def finish_kernel(*refs):
    ds_ref, dk_out, dv_out, dk_ref, dv_ref, sems = refs[-6:]
    pieces = refs[:-6]
    parts = len(pieces)
    wide = 2 * DEPTH
    for d, piece in enumerate(pieces):
        total = sum(ds_ref[c * parts + here(d)] for c in range(ds_ref.shape[0] // parts))
        full = (piece[...].astype(F32) + total * (1.0 / BLOCK)).astype(BF)
        cols = cols_of(here(d), wide)
        dk_ref[:, cols] = full[:, :wide]
        dv_ref[:, cols] = full[:, wide:]
    pairs = ((dk_ref, dk_out), (dv_ref, dv_out))
    run([pltpu.make_async_copy(a, b, sems.at[i]) for i, (a, b) in enumerate(pairs)])


def finish(pieces, ds):
    parts = len(pieces)
    rows = pieces[0].shape[0]
    shape = (rows, parts * 2 * DEPTH)
    return pl.pallas_call(
        finish_kernel,
        in_specs=[VM] * (parts + 1),
        out_specs=[HB] * 2,
        out_shape=[jax.ShapeDtypeStruct(shape, BF)] * 2,
        scratch_shapes=[pltpu.VMEM(shape, BF)] * 2 + [pltpu.SemaphoreType.DMA((2,))],
        compiler_params=ROOM,
        name="finish",
    )(*pieces, ds)


def swap(pieces):
    parts = len(pieces)
    moved = []
    for d in range(1, parts):
        pairs = [(i, i ^ d) for i in range(parts)]
        moved.append(lax.ppermute(pieces[d], "head", pairs))
    return [pieces[0]] + moved


def layer(queries, keys, values, cotangent):
    rows = queries.shape[0]
    parts = lax.axis_size("head")
    blocks = lax.axis_size("ctx")
    assert rows * parts == BLOCK and parts * 2 == KEY_VALUE_HEADS
    forth = [(i, i + 1) for i in range(blocks - 1)]
    back = [(i + 1, i) for i in range(blocks - 1)]
    queries, keys, values, cotangent = [
        pltpu.with_memory_space_constraint(x, pltpu.HBM)
        for x in (queries, keys, values, cotangent)
    ]
    kv = pack_kv(keys, values, parts)
    kv = swap(kv)
    pieces_a, pieces_b = pack(queries, cotangent, parts)
    pieces_a = swap(pieces_a)
    pieces_b = swap(pieces_b)
    kv_a, kv_b, sums = gather(kv, blocks)
    prev_a = lax.ppermute(kv_a, "ctx", forth)
    prev_b = lax.ppermute(kv_b, "ctx", forth)
    sums = lax.all_to_all(sums, "ctx", 0, 0, tiled=True)
    out_a, edge_a, own_a, ds_a = attend(pieces_a, kv_a, prev_a, sums, 0)
    out_a = swap(out_a)
    edge_a = lax.ppermute(edge_a, "ctx", back)
    out_b, edge_b, own_b, ds_b = attend(pieces_b, kv_b, prev_b, sums, 1)
    edge_b = lax.ppermute(edge_b, "ctx", back)
    out_b = swap(out_b)
    ds = spread(ds_a, ds_b, parts)
    ds = lax.all_to_all(ds, ("ctx", "head"), 0, 0, tiled=True)
    dkv = join((own_a, own_b), (edge_a, edge_b), parts)
    dkv = swap(dkv)
    out, grad_queries = unpack(out_a, out_b)
    grad_keys, grad_values = finish(dkv, ds)
    return out, grad_queries, grad_keys, grad_values


def solution(mesh):
    placed = P(("ctx", "head"), None)
    return jax.shard_map(
        layer, mesh=mesh, in_specs=(placed,) * 4, out_specs=(placed,) * 4, check_vma=False
    )
```

```python
import jax
import jax.numpy as jnp
from jax import lax
from jax.experimental import pallas as pl
from jax.experimental.pallas import tpu as pltpu
from jax.sharding import PartitionSpec as P


QUERY_HEADS = 32
KEY_VALUE_HEADS = 8
DEPTH = 128
BLOCK = 512
TILE = 256
GROUP = QUERY_HEADS // KEY_VALUE_HEADS
LOWEST = -1e30
LOG2E = 1.4426950408889634

BF = jnp.bfloat16
F32 = jnp.float32


def dot(a, b, ca, cb):
    return lax.dot_general(a, b, (((ca,), (cb,)), ((), ())), preferred_element_type=F32)


VM = pl.BlockSpec(memory_space=pltpu.VMEM)
HB = pl.BlockSpec(memory_space=pltpu.HBM)
ROOM = pltpu.CompilerParams(vmem_limit_bytes=12 << 20)


def here(d):
    return lax.axis_index("head") ^ d


def rows_of(d, size):
    return pl.ds(pl.multiple_of(here(d) * size, size), size)


def run(copies):
    for copy in copies:
        copy.start()
    for copy in copies:
        copy.wait()


def cols_of(start, size):
    return pl.ds(pl.multiple_of(start * size, size), size)


def pack_kv_kernel(k_ref, v_ref, *outs):
    sems, outs = outs[-1], outs[:-1]
    wide = 2 * DEPTH
    copies = []
    for d, out in enumerate(outs):
        cols = cols_of(here(d), wide)
        for i, ref in enumerate((k_ref, v_ref)):
            half = out.at[:, pl.ds(i * wide, wide)]
            copies.append(pltpu.make_async_copy(ref.at[:, cols], half, sems.at[2 * d + i]))
    run(copies)


def pack_kv(k, v, parts):
    rows = k.shape[0]
    return pl.pallas_call(
        pack_kv_kernel,
        in_specs=[HB] * 2,
        out_specs=[VM] * parts,
        out_shape=[jax.ShapeDtypeStruct((rows, 4 * DEPTH), BF)] * parts,
        scratch_shapes=[pltpu.SemaphoreType.DMA((2 * parts,))],
        compiler_params=ROOM,
        name="pack_kv",
    )(k, v)


def pack_kernel(q_ref, g_ref, *outs):
    sems, outs = outs[-1], outs[:-1]
    parts = len(outs) // 2
    copies = []
    for which in range(2):
        for d in range(parts):
            cols = cols_of(2 * here(d) + which, GROUP * DEPTH)
            for i, ref in enumerate((q_ref, g_ref)):
                out = outs[which * parts + d].at[i]
                copies.append(pltpu.make_async_copy(ref.at[:, cols], out, sems.at[len(copies)]))
    run(copies)


def pack(q, g, parts):
    outs = pl.pallas_call(
        pack_kernel,
        in_specs=[HB] * 2,
        out_specs=[VM] * (2 * parts),
        out_shape=[jax.ShapeDtypeStruct((2, q.shape[0], GROUP * DEPTH), BF)] * (2 * parts),
        scratch_shapes=[pltpu.SemaphoreType.DMA((4 * parts,))],
        compiler_params=ROOM,
        name="pack",
    )(q, g)
    return outs[:parts], outs[parts:]


def gather_kernel(*refs):
    a_ref, b_ref, sums_ref = refs[-3:]
    rows = refs[0].shape[0]
    total = jnp.zeros((1, 4 * DEPTH), F32)
    for d, piece in enumerate(refs[:-3]):
        at = rows_of(d, rows)
        for which, out in enumerate((a_ref, b_ref)):
            out[at, :DEPTH] = piece[:, which * DEPTH : (which + 1) * DEPTH]
            out[at, DEPTH:] = piece[:, (2 + which) * DEPTH : (3 + which) * DEPTH]
        total = total + jnp.sum(piece[...].astype(F32), axis=0, keepdims=True)
    for block in range(sums_ref.shape[0]):
        sums_ref[block] = total


def gather(pieces, blocks):
    return pl.pallas_call(
        gather_kernel,
        in_specs=[VM] * len(pieces),
        out_specs=[VM] * 3,
        out_shape=[jax.ShapeDtypeStruct((BLOCK, 2 * DEPTH), BF)] * 2
        + [jax.ShapeDtypeStruct((blocks, 1, 4 * DEPTH), F32)],
        compiler_params=ROOM,
        name="gather_kv",
    )(*pieces)


def unflatten(refs):
    return (*refs[:10], refs[10:12], refs[12:14], refs[14], refs[15])


def attend_kernel(parts, which, *refs):
    pieces = refs[:parts]
    kv_ref, prev_ref, sums_ref = refs[parts : parts + 3]
    outs = refs[parts + 3 : 2 * parts + 3]
    edge_ref, own_ref, ds_ref = refs[2 * parts + 3 : 2 * parts + 6]
    kc, vc, kt, vt, dk, dv, qs, gs, os, dqs, sbufs, lbufs, dbuf, tops = unflatten(refs[2 * parts + 6 :])
    ctx = lax.axis_index("ctx")
    scale = DEPTH ** (-0.5)
    coef = scale * LOG2E
    count = sums_ref.shape[0]
    pad = kc.shape[0] - 2 * BLOCK
    small = BLOCK // parts

    mean = jnp.concatenate([sums_ref[c] for c in range(count)], axis=0)
    mean = (mean * (1.0 / BLOCK)).astype(BF)
    if pad > count:
        mean = jnp.concatenate([mean, jnp.zeros((pad - count, 4 * DEPTH), BF)], axis=0)
    for part, (all_ref, tr) in enumerate(((kc, kt), (vc, vt))):
        cols = slice(part * DEPTH, (part + 1) * DEPTH)
        at = (2 * part + which) * DEPTH
        all_ref[:pad] = mean[:, at : at + DEPTH]
        all_ref[pad : pad + BLOCK] = prev_ref[:, cols]
        all_ref[pad + BLOCK :] = kv_ref[:, cols]
        tr[...] = all_ref[...].T
    dk[...] = jnp.zeros_like(dk)
    dv[...] = jnp.zeros_like(dv)

    def extent(tile):
        return pad + BLOCK + TILE * (tile + 1)

    def chunks(tile):
        cuts = [0] + list(range(pad + TILE, extent(tile) + 1, TILE))
        return list(zip(cuts[:-1], cuts[1:]))

    def fetch(head, slot):
        for d, piece in enumerate(pieces):
            at = rows_of(d, small)
            qs[slot, at, :] = piece[0, :, cols_of(head, DEPTH)]
            gs[slot, at, :] = piece[1, :, cols_of(head, DEPTH)]

    def rows_in(tile):
        return slice(tile * TILE, (tile + 1) * TILE)

    def scores(tile, slot):
        state = dict(own=jnp.full((1, TILE), LOWEST, F32), prev=jnp.full((1, TILE), LOWEST, F32))

        def part(lo, hi):
            def go():
                s = dot(kc[lo:hi], qs[slot, rows_in(tile), :], 1, 1)
                if lo == 0:
                    at = lax.broadcasted_iota(jnp.int32, (pad, TILE), 0)
                    first = jnp.where(at < ctx, s[:pad], LOWEST)
                    sbufs[tile][:pad] = first
                    state["own"] = jnp.maximum(state["own"], jnp.max(first, axis=0, keepdims=True))
                    s = s[pad:]
                if hi == extent(tile):
                    ki = lax.broadcasted_iota(jnp.int32, (TILE, TILE), 0)
                    qi = lax.broadcasted_iota(jnp.int32, (TILE, TILE), 1)
                    s = jnp.where(ki <= qi, s, LOWEST)
                sbufs[tile][max(lo, pad) : hi] = s
                name = "prev" if hi <= pad + BLOCK else "own"
                state[name] = jnp.maximum(state[name], jnp.max(s, axis=0, keepdims=True))
                if hi == extent(tile):
                    prev = jnp.where(ctx > 0, state["prev"], LOWEST)
                    tops[tile] = jnp.maximum(state["own"], prev)

            return go

        return [part(lo, hi) for lo, hi in chunks(tile)]

    def weigh(tile, state):
        def part(lo, hi):
            def go():
                top = tops[tile]
                behind = jnp.where(ctx > 0, top, -LOWEST)
                edges = [(lo, pad, top), (pad, hi, behind)] if lo == 0 else [
                    (lo, hi, behind if hi <= pad + BLOCK else top)
                ]
                for a, b, shift in edges:
                    w = jnp.exp2((sbufs[tile][a:b] - shift) * coef)
                    sbufs[tile][a:b] = w
                    lbufs[tile][a:b] = w.astype(BF)
                    total = jnp.sum(w, axis=0, keepdims=True)
                    state["total"] = total + state["total"] if "total" in state else total

            return go

        return [part(lo, hi) for lo, hi in chunks(tile)]

    def gradients(tile, state, slot):
        edge = extent(tile)
        rows = rows_in(tile)

        def out():
            inv = 1.0 / state["total"]
            attended = dot(vt[:, :edge], lbufs[tile][:edge], 1, 0) * inv
            os[rows, :] = attended.T.astype(BF)
            gt = (gs[slot, rows, :].astype(F32).T * (16.0 * inv)).astype(BF)
            state["gt"] = gt
            state["dot"] = jnp.sum(gt.astype(F32) * attended, axis=0, keepdims=True)

        def part(lo, hi):
            def go():
                back = dot(vc[lo:hi], state["gt"], 1, 0)
                dbuf[lo:hi] = (sbufs[tile][lo:hi] * (back - state["dot"])).astype(BF)

            return go

        def query():
            dqs[rows, :] = (dot(kt[:, :edge], dbuf[:edge], 1, 0) * scale).T.astype(BF)

        def store(lo, hi):
            def go():
                dv[lo:hi] += dot(lbufs[tile][lo:hi], state["gt"], 1, 1)
                dk[lo:hi] += dot(dbuf[lo:hi], qs[slot, rows, :], 1, 0)

            return go

        steps = [out] + [part(lo, hi) for lo, hi in chunks(tile)] + [query]
        return steps + [store(lo, hi) for lo, hi in chunks(tile)]

    def weave(*stages):
        order = []
        for n, stage in enumerate(stages):
            order += [((i + 0.5) / len(stage), n, i, go) for i, go in enumerate(stage)]
        for item in sorted(order, key=lambda x: x[:3]):
            item[3]()

    fetch(0, 0)
    weave(scores(0, 0))

    def step(head, carry):
        first, second = {}, {}
        slot = head % 2
        later = jnp.minimum(head + 1, GROUP - 1)
        weave(scores(1, slot), weigh(0, first))
        weave(weigh(1, second), gradients(0, first, slot))
        weave(gradients(1, second, slot), [lambda: fetch(later, 1 - slot)] + scores(0, 1 - slot))
        for d, out in enumerate(outs):
            at = rows_of(d, small)
            out[0, :, cols_of(head, DEPTH)] = os[at, :]
            out[1, :, cols_of(head, DEPTH)] = dqs[at, :]
        return carry

    lax.fori_loop(0, GROUP, step, 0)
    ds_ref[:, :DEPTH] = dk[:count] * scale
    ds_ref[:, DEPTH:] = dv[:count]
    edge_ref[:, :DEPTH] = (dk[pad : pad + BLOCK] * scale).astype(BF)
    edge_ref[:, DEPTH:] = dv[pad : pad + BLOCK].astype(BF)
    own_ref[:, :DEPTH] = dk[pad + BLOCK :] * scale
    own_ref[:, DEPTH:] = dv[pad + BLOCK :]


def attend(pieces, kv, prev, sums, which):
    parts = len(pieces)
    small = BLOCK // parts
    count = sums.shape[0]
    pad = max(16, -(-count // 16) * 16)
    width = pad + 2 * BLOCK
    outs = pl.pallas_call(
        lambda *refs: attend_kernel(parts, which, *refs),
        in_specs=[VM] * (parts + 3),
        out_specs=[VM] * (parts + 3),
        out_shape=[jax.ShapeDtypeStruct((2, small, GROUP * DEPTH), BF)] * parts
        + [
            jax.ShapeDtypeStruct((BLOCK, 2 * DEPTH), BF),
            jax.ShapeDtypeStruct((BLOCK, 2 * DEPTH), F32),
            jax.ShapeDtypeStruct((count, 2 * DEPTH), F32),
        ],
        scratch_shapes=[
            pltpu.VMEM((width, DEPTH), BF),
            pltpu.VMEM((width, DEPTH), BF),
            pltpu.VMEM((DEPTH, width), BF),
            pltpu.VMEM((DEPTH, width), BF),
            pltpu.VMEM((width, DEPTH), F32),
            pltpu.VMEM((width, DEPTH), F32),
            pltpu.VMEM((2, BLOCK, DEPTH), BF),
            pltpu.VMEM((2, BLOCK, DEPTH), BF),
            pltpu.VMEM((BLOCK, DEPTH), BF),
            pltpu.VMEM((BLOCK, DEPTH), BF),
            pltpu.VMEM((width - TILE, TILE), F32),
            pltpu.VMEM((width, TILE), F32),
            pltpu.VMEM((width - TILE, TILE), BF),
            pltpu.VMEM((width, TILE), BF),
            pltpu.VMEM((width, TILE), BF),
            pltpu.VMEM((2, 1, TILE), F32),
        ],
        compiler_params=pltpu.CompilerParams(vmem_limit_bytes=24 << 20),
        cost_estimate=pl.CostEstimate(
            flops=12 * GROUP * BLOCK * 2 * BLOCK * DEPTH,
            bytes_accessed=8 * BLOCK * GROUP * DEPTH,
            transcendentals=GROUP * BLOCK * 2 * BLOCK,
        ),
        name="attend",
    )(*pieces, kv, prev, sums)
    return outs[:parts], outs[parts], outs[parts + 1], outs[parts + 2]


def join_kernel(own_a, own_b, edge_a, edge_b, *outs):
    rows = outs[0].shape[0]
    for d, out in enumerate(outs):
        at = rows_of(d, rows)
        for g, (own, edge) in enumerate(((own_a, edge_a), (own_b, edge_b))):
            both = (own[at, :] + edge[at, :].astype(F32)).astype(BF)
            out[:, g * DEPTH : (g + 1) * DEPTH] = both[:, :DEPTH]
            out[:, (2 + g) * DEPTH : (3 + g) * DEPTH] = both[:, DEPTH:]


def join(own, edge, parts):
    return pl.pallas_call(
        join_kernel,
        in_specs=[VM] * 4,
        out_specs=[VM] * parts,
        out_shape=[jax.ShapeDtypeStruct((BLOCK // parts, 4 * DEPTH), BF)] * parts,
        compiler_params=ROOM,
        name="join",
    )(own[0], own[1], edge[0], edge[1])


def spread_kernel(a_ref, b_ref, out_ref):
    blocks = a_ref.shape[0]
    parts = out_ref.shape[0] // blocks
    for block in range(blocks):
        for g, ref in enumerate((a_ref, b_ref)):
            row = ref[block : block + 1, :]
            for i in range(2):
                at = (2 * i + g) * DEPTH
                part = row[:, i * DEPTH : (i + 1) * DEPTH]
                for h in range(parts):
                    out_ref[block * parts + h, :, at : at + DEPTH] = part


def spread(a, b, parts):
    return pl.pallas_call(
        spread_kernel,
        in_specs=[VM] * 2,
        out_specs=VM,
        out_shape=jax.ShapeDtypeStruct((a.shape[0] * parts, 1, 4 * DEPTH), F32),
        compiler_params=ROOM,
        name="spread",
    )(a, b)


def unpack_kernel(*refs):
    sems, outs, pieces = refs[-1], refs[-3:-1], refs[:-3]
    parts = len(pieces) // 2
    copies = []
    for n, piece in enumerate(pieces):
        cols = cols_of(2 * here(n % parts) + n // parts, GROUP * DEPTH)
        for i, out in enumerate(outs):
            copies.append(
                pltpu.make_async_copy(piece.at[i], out.at[:, cols], sems.at[len(copies)])
            )
    run(copies)


def unpack(a, b):
    parts = len(a)
    rows = a[0].shape[1]
    shape = jax.ShapeDtypeStruct((rows, parts * 2 * GROUP * DEPTH), BF)
    return pl.pallas_call(
        unpack_kernel,
        in_specs=[VM] * (2 * parts),
        out_specs=[HB] * 2,
        out_shape=[shape, shape],
        scratch_shapes=[pltpu.SemaphoreType.DMA((4 * parts,))],
        compiler_params=ROOM,
        name="unpack",
    )(*a, *b)


def finish_kernel(*refs):
    ds_ref, dk_out, dv_out, dk_ref, dv_ref, sems = refs[-6:]
    pieces = refs[:-6]
    parts = len(pieces)
    wide = 2 * DEPTH
    for d, piece in enumerate(pieces):
        total = sum(ds_ref[c * parts + here(d)] for c in range(ds_ref.shape[0] // parts))
        full = (piece[...].astype(F32) + total * (1.0 / BLOCK)).astype(BF)
        cols = cols_of(here(d), wide)
        dk_ref[:, cols] = full[:, :wide]
        dv_ref[:, cols] = full[:, wide:]
    pairs = ((dk_ref, dk_out), (dv_ref, dv_out))
    run([pltpu.make_async_copy(a, b, sems.at[i]) for i, (a, b) in enumerate(pairs)])


def finish(pieces, ds):
    parts = len(pieces)
    rows = pieces[0].shape[0]
    shape = (rows, parts * 2 * DEPTH)
    return pl.pallas_call(
        finish_kernel,
        in_specs=[VM] * (parts + 1),
        out_specs=[HB] * 2,
        out_shape=[jax.ShapeDtypeStruct(shape, BF)] * 2,
        scratch_shapes=[pltpu.VMEM(shape, BF)] * 2 + [pltpu.SemaphoreType.DMA((2,))],
        compiler_params=ROOM,
        name="finish",
    )(*pieces, ds)


def swap(pieces):
    parts = len(pieces)
    moved = []
    for d in range(1, parts):
        pairs = [(i, i ^ d) for i in range(parts)]
        moved.append(lax.ppermute(pieces[d], "head", pairs))
    return [pieces[0]] + moved


def layer(queries, keys, values, cotangent):
    rows = queries.shape[0]
    parts = lax.axis_size("head")
    blocks = lax.axis_size("ctx")
    assert rows * parts == BLOCK and parts * 2 == KEY_VALUE_HEADS
    forth = [(i, i + 1) for i in range(blocks - 1)]
    back = [(i + 1, i) for i in range(blocks - 1)]
    queries, keys, values, cotangent = [
        pltpu.with_memory_space_constraint(x, pltpu.HBM)
        for x in (queries, keys, values, cotangent)
    ]
    kv = pack_kv(keys, values, parts)
    kv = swap(kv)
    pieces_a, pieces_b = pack(queries, cotangent, parts)
    pieces_a = swap(pieces_a)
    pieces_b = swap(pieces_b)
    kv_a, kv_b, sums = gather(kv, blocks)
    prev_a = lax.ppermute(kv_a, "ctx", forth)
    prev_b = lax.ppermute(kv_b, "ctx", forth)
    sums = lax.all_to_all(sums, "ctx", 0, 0, tiled=True)
    out_a, edge_a, own_a, ds_a = attend(pieces_a, kv_a, prev_a, sums, 0)
    out_a = swap(out_a)
    edge_a = lax.ppermute(edge_a, "ctx", back)
    out_b, edge_b, own_b, ds_b = attend(pieces_b, kv_b, prev_b, sums, 1)
    edge_b = lax.ppermute(edge_b, "ctx", back)
    out_b = swap(out_b)
    ds = spread(ds_a, ds_b, parts)
    ds = lax.all_to_all(ds, ("ctx", "head"), 0, 0, tiled=True)
    dkv = join((own_a, own_b), (edge_a, edge_b), parts)
    dkv = swap(dkv)
    out, grad_queries = unpack(out_a, out_b)
    grad_keys, grad_values = finish(dkv, ds)
    return out, grad_queries, grad_keys, grad_values


def solution(mesh):
    placed = P(("ctx", "head"), None)
    return jax.shard_map(
        layer, mesh=mesh, in_specs=(placed,) * 4, out_specs=(placed,) * 4, check_vma=False
    )
```

```python
import jax
import jax.numpy as jnp
from jax import lax
from jax.experimental import pallas as pl
from jax.experimental.pallas import tpu as pltpu
from jax.sharding import PartitionSpec as P


QUERY_HEADS = 32
KEY_VALUE_HEADS = 8
DEPTH = 128
BLOCK = 512
TILE = 256
GROUP = QUERY_HEADS // KEY_VALUE_HEADS
LOWEST = -1e30
LOG2E = 1.4426950408889634

BF = jnp.bfloat16
F32 = jnp.float32


def dot(a, b, ca, cb):
    return lax.dot_general(a, b, (((ca,), (cb,)), ((), ())), preferred_element_type=F32)


VM = pl.BlockSpec(memory_space=pltpu.VMEM)
HB = pl.BlockSpec(memory_space=pltpu.HBM)
ROOM = pltpu.CompilerParams(vmem_limit_bytes=12 << 20)


def here(d):
    return lax.axis_index("head") ^ d


def rows_of(d, size):
    return pl.ds(pl.multiple_of(here(d) * size, size), size)


def run(copies):
    for copy in copies:
        copy.start()
    for copy in copies:
        copy.wait()


def cols_of(start, size):
    return pl.ds(pl.multiple_of(start * size, size), size)


def pack_kv_kernel(k_ref, v_ref, *outs):
    sems, outs = outs[-1], outs[:-1]
    wide = 2 * DEPTH
    copies = []
    for d, out in enumerate(outs):
        cols = cols_of(here(d), wide)
        for i, ref in enumerate((k_ref, v_ref)):
            half = out.at[:, pl.ds(i * wide, wide)]
            copies.append(pltpu.make_async_copy(ref.at[:, cols], half, sems.at[2 * d + i]))
    run(copies)


def pack_kv(k, v, parts):
    rows = k.shape[0]
    return pl.pallas_call(
        pack_kv_kernel,
        in_specs=[HB] * 2,
        out_specs=[VM] * parts,
        out_shape=[jax.ShapeDtypeStruct((rows, 4 * DEPTH), BF)] * parts,
        scratch_shapes=[pltpu.SemaphoreType.DMA((2 * parts,))],
        compiler_params=ROOM,
        name="pack_kv",
    )(k, v)


def pack_kernel(q_ref, g_ref, *outs):
    sems, outs = outs[-1], outs[:-1]
    parts = len(outs) // 2
    copies = []
    for which in range(2):
        for d in range(parts):
            cols = cols_of(2 * here(d) + which, GROUP * DEPTH)
            for i, ref in enumerate((q_ref, g_ref)):
                out = outs[which * parts + d].at[i]
                copies.append(pltpu.make_async_copy(ref.at[:, cols], out, sems.at[len(copies)]))
    run(copies)


def pack(q, g, parts):
    outs = pl.pallas_call(
        pack_kernel,
        in_specs=[HB] * 2,
        out_specs=[VM] * (2 * parts),
        out_shape=[jax.ShapeDtypeStruct((2, q.shape[0], GROUP * DEPTH), BF)] * (2 * parts),
        scratch_shapes=[pltpu.SemaphoreType.DMA((4 * parts,))],
        compiler_params=ROOM,
        name="pack",
    )(q, g)
    return outs[:parts], outs[parts:]


def gather_kernel(*refs):
    a_ref, b_ref, sums_ref = refs[-3:]
    rows = refs[0].shape[0]
    total = jnp.zeros((1, 4 * DEPTH), F32)
    for d, piece in enumerate(refs[:-3]):
        at = rows_of(d, rows)
        for which, out in enumerate((a_ref, b_ref)):
            out[at, :DEPTH] = piece[:, which * DEPTH : (which + 1) * DEPTH]
            out[at, DEPTH:] = piece[:, (2 + which) * DEPTH : (3 + which) * DEPTH]
        total = total + jnp.sum(piece[...].astype(F32), axis=0, keepdims=True)
    for block in range(sums_ref.shape[0]):
        sums_ref[block] = total


def gather(pieces, blocks):
    return pl.pallas_call(
        gather_kernel,
        in_specs=[VM] * len(pieces),
        out_specs=[VM] * 3,
        out_shape=[jax.ShapeDtypeStruct((BLOCK, 2 * DEPTH), BF)] * 2
        + [jax.ShapeDtypeStruct((blocks, 1, 4 * DEPTH), F32)],
        compiler_params=ROOM,
        name="gather_kv",
    )(*pieces)


def unflatten(refs):
    return (*refs[:10], refs[10:12], refs[12:14], refs[14], refs[15])


def attend_kernel(parts, which, *refs):
    pieces = refs[:parts]
    kv_ref, prev_ref, sums_ref = refs[parts : parts + 3]
    outs = refs[parts + 3 : 2 * parts + 3]
    edge_ref, own_ref, ds_ref = refs[2 * parts + 3 : 2 * parts + 6]
    kc, vc, kt, vt, dk, dv, qs, gs, os, dqs, sbufs, lbufs, dbuf, tops = unflatten(refs[2 * parts + 6 :])
    ctx = lax.axis_index("ctx")
    scale = DEPTH ** (-0.5)
    coef = scale * LOG2E
    count = sums_ref.shape[0]
    pad = kc.shape[0] - 2 * BLOCK
    small = BLOCK // parts

    mean = jnp.concatenate([sums_ref[c] for c in range(count)], axis=0)
    mean = (mean * (1.0 / BLOCK)).astype(BF)
    if pad > count:
        mean = jnp.concatenate([mean, jnp.zeros((pad - count, 4 * DEPTH), BF)], axis=0)
    for part, (all_ref, tr) in enumerate(((kc, kt), (vc, vt))):
        cols = slice(part * DEPTH, (part + 1) * DEPTH)
        at = (2 * part + which) * DEPTH
        all_ref[:pad] = mean[:, at : at + DEPTH]
        all_ref[pad : pad + BLOCK] = prev_ref[:, cols]
        all_ref[pad + BLOCK :] = kv_ref[:, cols]
        tr[...] = all_ref[...].T
    dk[...] = jnp.zeros_like(dk)
    dv[...] = jnp.zeros_like(dv)

    def extent(tile):
        return pad + BLOCK + TILE * (tile + 1)

    def chunks(tile):
        cuts = [0] + list(range(pad + TILE, extent(tile) + 1, TILE))
        return list(zip(cuts[:-1], cuts[1:]))

    def fetch(head, slot):
        for d, piece in enumerate(pieces):
            at = rows_of(d, small)
            qs[slot, at, :] = piece[0, :, cols_of(head, DEPTH)]
            gs[slot, at, :] = piece[1, :, cols_of(head, DEPTH)]

    def rows_in(tile):
        return slice(tile * TILE, (tile + 1) * TILE)

    def scores(tile, slot):
        state = dict(own=jnp.full((1, TILE), LOWEST, F32), prev=jnp.full((1, TILE), LOWEST, F32))

        def part(lo, hi):
            def go():
                s = dot(kc[lo:hi], qs[slot, rows_in(tile), :], 1, 1)
                if lo == 0:
                    at = lax.broadcasted_iota(jnp.int32, (pad, TILE), 0)
                    first = jnp.where(at < ctx, s[:pad], LOWEST)
                    sbufs[tile][:pad] = first
                    state["own"] = jnp.maximum(state["own"], jnp.max(first, axis=0, keepdims=True))
                    s = s[pad:]
                if hi == extent(tile):
                    ki = lax.broadcasted_iota(jnp.int32, (TILE, TILE), 0)
                    qi = lax.broadcasted_iota(jnp.int32, (TILE, TILE), 1)
                    s = jnp.where(ki <= qi, s, LOWEST)
                sbufs[tile][max(lo, pad) : hi] = s
                name = "prev" if hi <= pad + BLOCK else "own"
                state[name] = jnp.maximum(state[name], jnp.max(s, axis=0, keepdims=True))
                if hi == extent(tile):
                    prev = jnp.where(ctx > 0, state["prev"], LOWEST)
                    tops[tile] = jnp.maximum(state["own"], prev)

            return go

        return [part(lo, hi) for lo, hi in chunks(tile)]

    def weigh(tile, state):
        def part(lo, hi):
            def go():
                top = tops[tile]
                behind = jnp.where(ctx > 0, top, -LOWEST)
                edges = [(lo, pad, top), (pad, hi, behind)] if lo == 0 else [
                    (lo, hi, behind if hi <= pad + BLOCK else top)
                ]
                for a, b, shift in edges:
                    w = jnp.exp2((sbufs[tile][a:b] - shift) * coef)
                    sbufs[tile][a:b] = w
                    lbufs[tile][a:b] = w.astype(BF)
                    total = jnp.sum(w, axis=0, keepdims=True)
                    state["total"] = total + state["total"] if "total" in state else total

            return go

        return [part(lo, hi) for lo, hi in chunks(tile)]

    def gradients(tile, state, slot):
        edge = extent(tile)
        rows = rows_in(tile)

        def out():
            inv = 1.0 / state["total"]
            attended = dot(vt[:, :edge], lbufs[tile][:edge], 1, 0) * inv
            os[rows, :] = attended.T.astype(BF)
            gt = (gs[slot, rows, :].astype(F32).T * (16.0 * inv)).astype(BF)
            state["gt"] = gt
            state["dot"] = jnp.sum(gt.astype(F32) * attended, axis=0, keepdims=True)

        def part(lo, hi):
            def go():
                back = dot(vc[lo:hi], state["gt"], 1, 0)
                dbuf[lo:hi] = (sbufs[tile][lo:hi] * (back - state["dot"])).astype(BF)

            return go

        def query():
            dqs[rows, :] = (dot(kt[:, :edge], dbuf[:edge], 1, 0) * scale).T.astype(BF)

        def store(lo, hi):
            def go():
                dk[lo:hi] += dot(dbuf[lo:hi], qs[slot, rows, :], 1, 0)

            return go

        steps = [out] + [part(lo, hi) for lo, hi in chunks(tile)] + [query]

        def values():
            dv[:edge] += dot(lbufs[tile][:edge], state["gt"], 1, 1)

        steps.insert(1, values)
        return steps + [store(lo, hi) for lo, hi in chunks(tile)]

    def weave(*stages):
        order = []
        for n, stage in enumerate(stages):
            order += [((i + 0.5) / len(stage), n, i, go) for i, go in enumerate(stage)]
        for item in sorted(order, key=lambda x: x[:3]):
            item[3]()

    fetch(0, 0)
    weave(scores(0, 0))

    def step(head, carry):
        first, second = {}, {}
        slot = head % 2
        later = jnp.minimum(head + 1, GROUP - 1)
        weave(scores(1, slot), weigh(0, first))
        weave(weigh(1, second), gradients(0, first, slot))
        weave(gradients(1, second, slot), [lambda: fetch(later, 1 - slot)] + scores(0, 1 - slot))
        for d, out in enumerate(outs):
            at = rows_of(d, small)
            out[0, :, cols_of(head, DEPTH)] = os[at, :]
            out[1, :, cols_of(head, DEPTH)] = dqs[at, :]
        return carry

    lax.fori_loop(0, GROUP, step, 0)
    ds_ref[:, :DEPTH] = dk[:count] * scale
    ds_ref[:, DEPTH:] = dv[:count]
    edge_ref[:, :DEPTH] = (dk[pad : pad + BLOCK] * scale).astype(BF)
    edge_ref[:, DEPTH:] = dv[pad : pad + BLOCK].astype(BF)
    own_ref[:, :DEPTH] = (dk[pad + BLOCK :] * scale).astype(BF)
    own_ref[:, DEPTH:] = dv[pad + BLOCK :].astype(BF)


def attend(pieces, kv, prev, sums, which):
    parts = len(pieces)
    small = BLOCK // parts
    count = sums.shape[0]
    pad = max(16, -(-count // 16) * 16)
    width = pad + 2 * BLOCK
    outs = pl.pallas_call(
        lambda *refs: attend_kernel(parts, which, *refs),
        in_specs=[VM] * (parts + 3),
        out_specs=[VM] * (parts + 3),
        out_shape=[jax.ShapeDtypeStruct((2, small, GROUP * DEPTH), BF)] * parts
        + [
            jax.ShapeDtypeStruct((BLOCK, 2 * DEPTH), BF),
            jax.ShapeDtypeStruct((BLOCK, 2 * DEPTH), BF),
            jax.ShapeDtypeStruct((count, 2 * DEPTH), F32),
        ],
        scratch_shapes=[
            pltpu.VMEM((width, DEPTH), BF),
            pltpu.VMEM((width, DEPTH), BF),
            pltpu.VMEM((DEPTH, width), BF),
            pltpu.VMEM((DEPTH, width), BF),
            pltpu.VMEM((width, DEPTH), F32),
            pltpu.VMEM((width, DEPTH), F32),
            pltpu.VMEM((2, BLOCK, DEPTH), BF),
            pltpu.VMEM((2, BLOCK, DEPTH), BF),
            pltpu.VMEM((BLOCK, DEPTH), BF),
            pltpu.VMEM((BLOCK, DEPTH), BF),
            pltpu.VMEM((width - TILE, TILE), F32),
            pltpu.VMEM((width, TILE), F32),
            pltpu.VMEM((width - TILE, TILE), BF),
            pltpu.VMEM((width, TILE), BF),
            pltpu.VMEM((width, TILE), BF),
            pltpu.VMEM((2, 1, TILE), F32),
        ],
        compiler_params=pltpu.CompilerParams(vmem_limit_bytes=24 << 20),
        cost_estimate=pl.CostEstimate(
            flops=12 * GROUP * BLOCK * 2 * BLOCK * DEPTH,
            bytes_accessed=8 * BLOCK * GROUP * DEPTH,
            transcendentals=GROUP * BLOCK * 2 * BLOCK,
        ),
        name="attend",
    )(*pieces, kv, prev, sums)
    return outs[:parts], outs[parts], outs[parts + 1], outs[parts + 2]


def join_kernel(own, edge, *outs):
    rows = outs[0].shape[0]
    for d, out in enumerate(outs):
        at = rows_of(d, rows)
        out[...] = (own[at, :].astype(F32) + edge[at, :].astype(F32)).astype(BF)


def join(own, edge, parts):
    return pl.pallas_call(
        join_kernel,
        in_specs=[VM] * 2,
        out_specs=[VM] * parts,
        out_shape=[jax.ShapeDtypeStruct((BLOCK // parts, 2 * DEPTH), BF)] * parts,
        compiler_params=ROOM,
        name="join",
    )(own, edge)


def spread_kernel(a_ref, b_ref, out_ref):
    blocks = a_ref.shape[0]
    parts = out_ref.shape[0] // blocks
    for block in range(blocks):
        for g, ref in enumerate((a_ref, b_ref)):
            row = ref[block : block + 1, :]
            for i in range(2):
                at = (2 * i + g) * DEPTH
                part = row[:, i * DEPTH : (i + 1) * DEPTH]
                for h in range(parts):
                    out_ref[block * parts + h, :, at : at + DEPTH] = part


def spread(a, b, parts):
    return pl.pallas_call(
        spread_kernel,
        in_specs=[VM] * 2,
        out_specs=VM,
        out_shape=jax.ShapeDtypeStruct((a.shape[0] * parts, 1, 4 * DEPTH), F32),
        compiler_params=ROOM,
        name="spread",
    )(a, b)


def unpack_kernel(*refs):
    sems, outs, pieces = refs[-1], refs[-3:-1], refs[:-3]
    parts = len(pieces) // 2
    copies = []
    for n, piece in enumerate(pieces):
        cols = cols_of(2 * here(n % parts) + n // parts, GROUP * DEPTH)
        for i, out in enumerate(outs):
            copies.append(
                pltpu.make_async_copy(piece.at[i], out.at[:, cols], sems.at[len(copies)])
            )
    run(copies)


def unpack(a, b):
    parts = len(a)
    rows = a[0].shape[1]
    shape = jax.ShapeDtypeStruct((rows, parts * 2 * GROUP * DEPTH), BF)
    return pl.pallas_call(
        unpack_kernel,
        in_specs=[VM] * (2 * parts),
        out_specs=[HB] * 2,
        out_shape=[shape, shape],
        scratch_shapes=[pltpu.SemaphoreType.DMA((4 * parts,))],
        compiler_params=ROOM,
        name="unpack",
    )(*a, *b)


def finish_kernel(*refs):
    ds_ref, dk_out, dv_out, dk_ref, dv_ref, sems = refs[-6:]
    pieces = refs[:-6]
    parts = len(pieces) // 2
    for d in range(parts):
        total = sum(ds_ref[c * parts + here(d)] for c in range(ds_ref.shape[0] // parts))
        total = total * (1.0 / BLOCK)
        for g in range(2):
            piece = pieces[g * parts + d]
            cols = cols_of(2 * here(d) + g, DEPTH)
            for i, ref in enumerate((dk_ref, dv_ref)):
                spread = total[:, (2 * i + g) * DEPTH : (2 * i + g + 1) * DEPTH]
                half = piece[:, i * DEPTH : (i + 1) * DEPTH].astype(F32)
                ref[:, cols] = (half + spread).astype(BF)
    pairs = ((dk_ref, dk_out), (dv_ref, dv_out))
    run([pltpu.make_async_copy(a, b, sems.at[i]) for i, (a, b) in enumerate(pairs)])


def finish(a, b, ds):
    parts = len(a)
    shape = (a[0].shape[0], parts * 2 * DEPTH)
    return pl.pallas_call(
        finish_kernel,
        in_specs=[VM] * (2 * parts + 1),
        out_specs=[HB] * 2,
        out_shape=[jax.ShapeDtypeStruct(shape, BF)] * 2,
        scratch_shapes=[pltpu.VMEM(shape, BF)] * 2 + [pltpu.SemaphoreType.DMA((2,))],
        compiler_params=ROOM,
        name="finish",
    )(*a, *b, ds)


def swap(pieces):
    parts = len(pieces)
    moved = []
    for d in range(1, parts):
        pairs = [(i, i ^ d) for i in range(parts)]
        moved.append(lax.ppermute(pieces[d], "head", pairs))
    return [pieces[0]] + moved


def layer(queries, keys, values, cotangent):
    rows = queries.shape[0]
    parts = lax.axis_size("head")
    blocks = lax.axis_size("ctx")
    assert rows * parts == BLOCK and parts * 2 == KEY_VALUE_HEADS
    forth = [(i, i + 1) for i in range(blocks - 1)]
    back = [(i + 1, i) for i in range(blocks - 1)]
    queries, keys, values, cotangent = [
        pltpu.with_memory_space_constraint(x, pltpu.HBM)
        for x in (queries, keys, values, cotangent)
    ]
    kv = pack_kv(keys, values, parts)
    kv = swap(kv)
    pieces_a, pieces_b = pack(queries, cotangent, parts)
    pieces_a = swap(pieces_a)
    pieces_b = swap(pieces_b)
    kv_a, kv_b, sums = gather(kv, blocks)
    prev_a = lax.ppermute(kv_a, "ctx", forth)
    prev_b = lax.ppermute(kv_b, "ctx", forth)
    sums = lax.all_to_all(sums, "ctx", 0, 0, tiled=True)
    out_a, edge_a, own_a, ds_a = attend(pieces_a, kv_a, prev_a, sums, 0)
    out_a = swap(out_a)
    edge_a = lax.ppermute(edge_a, "ctx", back)
    out_b, edge_b, own_b, ds_b = attend(pieces_b, kv_b, prev_b, sums, 1)
    edge_b = lax.ppermute(edge_b, "ctx", back)
    out_b = swap(out_b)
    ds = spread(ds_a, ds_b, parts)
    ds = lax.all_to_all(ds, ("ctx", "head"), 0, 0, tiled=True)
    dkv_a = join(own_a, edge_a, parts)
    dkv_a = swap(dkv_a)
    dkv_b = join(own_b, edge_b, parts)
    dkv_b = swap(dkv_b)
    out, grad_queries = unpack(out_a, out_b)
    grad_keys, grad_values = finish(dkv_a, dkv_b, ds)
    return out, grad_queries, grad_keys, grad_values


def solution(mesh):
    placed = P(("ctx", "head"), None)
    return jax.shard_map(
        layer, mesh=mesh, in_specs=(placed,) * 4, out_specs=(placed,) * 4, check_vma=False
    )
```
